32 devices in a mesh: ctx: 8 (over z, x), head: 4 (over y, core).
Axes of the slice: x: 2, y: 2, z: 4, core: 2. Of those that a mesh axis runs over, the one named last changes fastest.
Arguments:
- query_raw: bfloat16 [16384, 2048], P(('ctx', 'head')), may hold values from -6 to 6
- key_raw: bfloat16 [16384, 2048], P(('ctx', 'head')), may hold values from -6 to 6
- values: bfloat16 [16384, 4096], P(('ctx', 'head')), may hold values from -48 to 48
- in_gate: bfloat16 [16384, 8], P(('ctx', 'head')), may hold values from -10 to 130
- forget_gate: bfloat16 [16384, 8], P(('ctx', 'head')), may hold values from -1 to 16
- query_conv: bfloat16 [4, 2048], replicated, may hold values from -3 to 3
- key_conv: bfloat16 [4, 2048], replicated, may hold values from -3 to 3
Outputs:
- hidden_out: bfloat16 [16384, 4096], P(('ctx', 'head'))
The draws below stay inside these ranges and needn't reach their ends.
All inputs are finite; a program needn't handle non-finite values.
Results may differ from the reference program's by a relative error of at most 0.0052.
Values may be sent and summed in bfloat16 or wider, within the bound.
No kernel may reach another device: no remote copies, remote signals or barrier semaphores. Data moves between devices by JAX's collectives and lax.ppermute only.
A program may use at most 192 MiB of HBM per device.

```python
import math
import jax
import jax.numpy as jnp
from jax import lax

HEAD_TOTAL = 8
DK = 256
DV = 512
CONV = 4
BLK = 512
TOK_DEV = 2048
QK = 2048
VD = 4096
TOKEN_TOTAL = 16384


def draw_forget_gate(key, part):
    key = jax.random.fold_in(key, 31)
    key_sequence, key_portion, key_coarse, key_location, key_sudden = jax.random.split(key, 5)
    ranking = jax.random.permutation(key_sequence, HEAD_TOTAL)
    fast_heads = ranking < HEAD_TOTAL // 2
    base_rate = jnp.where(fast_heads, jnp.float32(1.0 / 40.0), jnp.float32(0.5 / TOKEN_TOTAL))
    segment_scale = jnp.exp(jax.random.uniform(key_portion, (TOKEN_TOTAL // TOK_DEV, HEAD_TOTAL), jnp.float32, math.log(0.5), math.log(2.0)))
    segment_full = jnp.repeat(segment_scale, TOK_DEV, axis=0)
    rough_scale = jnp.exp(jax.random.uniform(key_coarse, (TOKEN_TOTAL, HEAD_TOTAL), jnp.float32, math.log(0.5), math.log(2.0)))
    rate = base_rate[None, :] * segment_full * rough_scale
    places = jax.random.randint(key_location, (3, HEAD_TOTAL), 0, TOKEN_TOTAL)
    positions = jnp.arange(TOKEN_TOTAL)
    struck = jnp.any(places[:, None, :] == positions[None, :, None], axis=0)
    dropped_fraction = jax.random.uniform(key_sudden, (TOKEN_TOTAL, HEAD_TOTAL), jnp.float32, 0.2, 0.5)
    rate = jnp.where(struck, -jnp.log(1.0 - dropped_fraction), rate)
    return (-jnp.log(jnp.expm1(rate))).astype(jnp.bfloat16)


def draw_in_gate(key, part):
    key = jax.random.fold_in(key, 47)
    key_base = jax.random.fold_in(key, 0)
    result = -4.0 + 1.5 * jax.random.truncated_normal(key_base, -4.0, 4.0, (TOKEN_TOTAL, HEAD_TOTAL), jnp.float32)
    return result.astype(jnp.bfloat16)


def draw_values(key, part):
    key = jax.random.fold_in(key, 59)
    key_noise = jax.random.fold_in(key, 0)
    key_rows = jax.random.fold_in(key, 2)
    key_columns = jax.random.fold_in(key, 3)
    noise = jax.random.truncated_normal(key_noise, -5.0, 5.0, (TOKEN_TOTAL, VD), jnp.float32)
    row_scale = jnp.exp(jax.random.uniform(key_rows, (TOKEN_TOTAL, 1), jnp.float32, math.log(0.3), math.log(3.0)))
    column_scale = jnp.exp(jax.random.uniform(key_columns, (1, VD), jnp.float32, math.log(0.3), math.log(3.0)))
    result = noise * row_scale * column_scale
    return result.astype(jnp.bfloat16)


def steps_of(key, extent, shards, low, high):
    def one(dim, shards_of):
        steps = jax.random.uniform(jax.random.fold_in(jax.random.fold_in(key, 6), dim), (shards_of,), jnp.float32, low / len(shards), high / len(shards))
        return jnp.repeat(jnp.exp(steps), extent[dim] // shards_of).reshape((-1,) + (1,) * (len(extent) - dim - 1))

    gain = one(*shards[0])
    for cut in shards[1:]:
        gain = gain * one(*cut)
    return gain


def bell_draw(key, dims, spread, most, shards=(), held_as=jnp.bfloat16):
    entries = jax.random.normal(key, dims, jnp.float32) * spread
    if len(shards) > 0:
        entries = steps_of(key, dims, shards, -0.22, 0.18) * entries
    return jnp.clip(entries, min=-most, max=most).astype(held_as)


def setup_inputs(seed: int = 0) -> dict:
    seeds = jax.random.split(jax.random.key(seed), 8)
    return {
        "query_raw": bell_draw(seeds[0], (TOKEN_TOTAL, QK), 1.0, 6.0, ((0, 32),)),
        "key_raw": bell_draw(seeds[1], (TOKEN_TOTAL, QK), 1.0, 6.0, ((0, 32),)),
        "values": draw_values(jax.random.fold_in(seeds[7], 71), 0),
        "in_gate": draw_in_gate(jax.random.fold_in(seeds[7], 71), 0),
        "forget_gate": draw_forget_gate(jax.random.fold_in(seeds[7], 71), 0),
        "query_conv": bell_draw(seeds[5], (CONV, QK), CONV ** -0.5, 3.0),
        "key_conv": bell_draw(seeds[6], (CONV, QK), CONV ** -0.5, 3.0),
    }


def conv_silu(raw_rows, conv_weight):
    row_count = raw_rows.shape[0]
    padded = jnp.concatenate([jnp.zeros((CONV - 1, raw_rows.shape[1]), jnp.float32), raw_rows.astype(jnp.float32)], axis=0)
    mixed = jnp.zeros(raw_rows.shape, jnp.float32)
    for offset in range(CONV):
        mixed = mixed + conv_weight[offset].astype(jnp.float32)[None, :] * padded[offset:offset + row_count]
    return jax.nn.silu(mixed).astype(jnp.bfloat16)


def block_step(carried, block_data):
    state_memory, state_norm, state_top = carried
    query_rows, key_rows, value_rows, gate_log, forget_log = block_data
    score_scale = DK ** -0.5
    forget_sum = jnp.cumsum(forget_log, axis=0)
    length = forget_sum.shape[0]
    causal = jnp.arange(length)[:, None] >= jnp.arange(length)[None, :]
    exponent = forget_sum[:, None, :] - forget_sum[None, :, :] + gate_log[None, :, :]
    exponent = jnp.where(causal[:, :, None], exponent, -jnp.inf)
    row_top = jnp.max(exponent, axis=1)
    weights = jnp.exp(exponent - row_top[:, None, :])
    query_wide = query_rows.astype(jnp.float32)
    key_wide = key_rows.astype(jnp.float32)
    value_wide = value_rows.astype(jnp.float32)
    scores = jnp.einsum('thd,shd->tsh', query_wide, key_wide) * score_scale
    mixing = (scores * weights).astype(jnp.bfloat16)
    near_num = jnp.einsum('tsh,she->the', mixing.astype(jnp.float32), value_wide)
    near_den = jnp.sum(mixing.astype(jnp.float32), axis=1)
    scaled = query_wide * score_scale
    far_num = jnp.einsum('thd,hde->the', scaled, state_memory, precision=lax.Precision.HIGHEST)
    far_den = jnp.einsum('thd,hd->th', scaled, state_norm, precision=lax.Precision.HIGHEST)
    far_log = forget_sum + state_top[None, :]
    row_peak = jnp.maximum(row_top, far_log)
    near_part = jnp.exp(row_top - row_peak)
    far_part = jnp.exp(far_log - row_peak)
    numerator = near_part[..., None] * near_num + far_part[..., None] * far_num
    denominator = near_part * near_den + far_part * far_den
    hidden = numerator / jnp.maximum(jnp.abs(denominator), 1.0)[..., None]
    total_log = forget_sum[-1]
    decay_log = total_log[None, :] - forget_sum + gate_log
    new_top = jnp.maximum(total_log + state_top, jnp.max(decay_log, axis=0))
    kept = jnp.exp(total_log + state_top - new_top)
    row_weight = jnp.exp(decay_log - new_top[None, :])
    weighted_keys = key_wide * row_weight[:, :, None]
    new_memory = kept[:, None, None] * state_memory + jnp.einsum('shd,she->hde', weighted_keys, value_wide, precision=lax.Precision.HIGHEST)
    new_norm = kept[:, None] * state_norm + jnp.sum(weighted_keys, axis=0)
    return (new_memory, new_norm, new_top), hidden.astype(jnp.bfloat16)


def reference(query_raw, key_raw, values, in_gate, forget_gate, query_conv, key_conv):
    query_act = conv_silu(query_raw, query_conv)
    key_act = conv_silu(key_raw, key_conv)
    blocks = TOKEN_TOTAL // BLK
    query_blocks = query_act.reshape(blocks, BLK, HEAD_TOTAL, DK)
    key_blocks = key_act.reshape(blocks, BLK, HEAD_TOTAL, DK)
    value_blocks = values.reshape(blocks, BLK, HEAD_TOTAL, DV)
    gate_blocks = in_gate.astype(jnp.float32).reshape(blocks, BLK, HEAD_TOTAL)
    forget_blocks = jax.nn.log_sigmoid(forget_gate.astype(jnp.float32)).reshape(blocks, BLK, HEAD_TOTAL)
    start_state = (jnp.zeros((HEAD_TOTAL, DK, DV), jnp.float32), jnp.zeros((HEAD_TOTAL, DK), jnp.float32), jnp.full((HEAD_TOTAL,), -1e30, jnp.float32))
    final_state, hidden = lax.scan(block_step, start_state, (query_blocks, key_blocks, value_blocks, gate_blocks, forget_blocks))
    return hidden.reshape(TOKEN_TOTAL, HEAD_TOTAL * DV)
```

```python
import functools

import jax
import jax.numpy as jnp
from jax import lax
from jax.experimental import pallas as pl
from jax.experimental.pallas import tpu as pltpu
from jax.sharding import PartitionSpec as P

AXES = ("ctx", "head")
HEADS = 8
GROUP = 4
DK = 256
DV = 512
HALF = 256
AUX = 16
ROWS = DK + AUX
BLK = 512
TAPS = 4
TILE = 256
STEP = 128
EMPTY = -1e30
SCALE = DK**-0.5
F32 = jnp.float32
BF16 = jnp.bfloat16


def narrow(x):
    return x.astype(BF16).astype(F32)


def split3(x):
    top = narrow(x)
    middle = narrow(x - top)
    return top, middle, x - top - middle


def aux_rows(norm, top, decay):
    norm_high = narrow(norm)
    parts = (norm_high, norm - norm_high) + split3(top) + split3(decay)
    row = lax.broadcasted_iota(jnp.int32, (AUX, HALF), 0)
    out = jnp.zeros((AUX, HALF), F32)
    for index, part in enumerate(parts):
        out = jnp.where(row == index, part, out)
    return out.astype(BF16)


def read_aux(aux):
    aux = aux.astype(F32)
    norm = aux[0:1] + aux[1:2]
    top = aux[2:3] + aux[3:4] + aux[4:5]
    decay = aux[5:6] + aux[6:7] + aux[7:8]
    return norm, top, decay


def column(ref, lane):
    lanes = lax.broadcasted_iota(jnp.int32, ref.shape, 1)
    return jnp.sum(jnp.where(lanes == lane, ref[...], 0.0), axis=1, keepdims=True)


def gates_kernel(in_ref, forget_ref, rows_ref, cols_ref):
    pad = jnp.zeros((BLK, 128 - HEADS), F32)

    def wide(x):
        return jnp.concatenate([x.astype(F32), pad], axis=1).T[:HEADS]

    gate = wide(in_ref[...])
    forget = wide(forget_ref[...])
    log_forget = jnp.minimum(forget, 0.0) - jnp.log1p(jnp.exp(-jnp.abs(forget)))
    lane = lax.broadcasted_iota(jnp.int32, (HEADS, BLK), 1)
    total = log_forget
    shift = 1
    while shift < BLK:
        total = total + jnp.where(lane >= shift, pltpu.roll(total, shift, 1), 0.0)
        shift *= 2
    level = gate - total
    top = level
    shift = 1
    while shift < BLK:
        top = jnp.maximum(top, jnp.where(lane >= shift, pltpu.roll(top, shift, 1), -jnp.inf))
        shift *= 2
    last_top = top[:, BLK - 1 :]
    last_total = total[:, BLK - 1 :]
    rows_ref[0:HEADS] = level
    rows_ref[HEADS : 2 * HEADS] = jnp.broadcast_to(last_total + last_top, (HEADS, BLK))
    rows_ref[2 * HEADS : 3 * HEADS] = jnp.broadcast_to(last_total, (HEADS, BLK))
    weight = jnp.exp(level - last_top)
    stacked = jnp.concatenate([top, weight, jnp.zeros((128 - 2 * HEADS, BLK), F32)], axis=0)
    cols_ref[...] = stacked.T


def gates(in_gate, forget_gate):
    return pl.pallas_call(
        gates_kernel,
        out_shape=(
            jax.ShapeDtypeStruct((3 * HEADS, BLK), F32),
            jax.ShapeDtypeStruct((BLK, 128), F32),
        ),
        name="gates",
    )(in_gate, forget_gate)


def conv_rows(raw_ref, rim_ref, tap_ref, padded):
    padded[0:8] = rim_ref[...].astype(F32)[8:16]
    padded[8 : 8 + BLK] = raw_ref[...].astype(F32)
    taps = tap_ref[...].astype(F32)
    for start in range(0, BLK, STEP):
        first = 8 - (TAPS - 1) + start
        mixed = taps[0:1] * padded[first : first + STEP]
        for tap in range(1, TAPS):
            mixed = mixed + taps[tap : tap + 1] * padded[first + tap : first + tap + STEP]
        yield start, (mixed * (0.5 * jnp.tanh(0.5 * mixed) + 0.5)).astype(BF16)


def query_kernel(raw_ref, rim_ref, tap_ref, out_ref, padded):
    for start, act in conv_rows(raw_ref, rim_ref, tap_ref, padded):
        out_ref[start : start + STEP] = act


def query_conv_act(raw, rim, taps):
    spec = lambda rows: pl.BlockSpec((rows, DK), lambda s: (0, s))
    return pl.pallas_call(
        query_kernel,
        grid=(HEADS,),
        in_specs=[spec(BLK), spec(16), spec(TAPS)],
        out_specs=spec(BLK),
        out_shape=jax.ShapeDtypeStruct(raw.shape, BF16),
        scratch_shapes=[pltpu.VMEM((BLK + 8, DK), F32)],
        name="query_conv",
    )(raw, rim, taps)


def block_state(base_ref, raw_ref, rim_ref, tap_ref, val_ref, rows_ref, cols_ref, act_ref, padded, weighted):
    head = base_ref[0] + pl.program_id(0)
    weight = column(cols_ref, HEADS + head)
    norm = jnp.zeros((1, DK), F32)
    for start, act in conv_rows(raw_ref, rim_ref, tap_ref, padded):
        act_ref[start : start + STEP] = act
        scaled = act.astype(F32) * weight[start : start + STEP]
        norm = norm + jnp.sum(scaled, axis=0, keepdims=True)
        weighted[start : start + STEP] = scaled.astype(BF16)
    memory = lax.dot_general(
        weighted[...], val_ref[...], (((0,), (0,)), ((), ())), preferred_element_type=F32
    )
    top = rows_ref[pl.ds(HEADS + head, 1), 0:HALF]
    decay = rows_ref[pl.ds(2 * HEADS + head, 1), 0:HALF]
    return memory, norm, top, decay


def write_record(ref, memory, norm, top, decay):
    aux = aux_rows(norm, top, decay)
    for half in range(DV // HALF):
        ref[half, 0:DK] = memory[:, half * HALF : (half + 1) * HALF].astype(BF16)
        ref[half, DK:ROWS] = aux


def send_kernel(base_ref, raw_ref, rim_ref, tap_ref, val_ref, rows_ref, cols_ref, rec_ref, act_ref, padded, weighted):
    state = block_state(
        base_ref, raw_ref, rim_ref, tap_ref, val_ref, rows_ref, cols_ref, act_ref, padded, weighted
    )
    write_record(rec_ref, *state)


def pair_kernel(
    base_ref, raw_ref, rim_ref, tap_ref, val_ref, rows_ref, cols_ref, other_ref,
    rec_ref, act_ref, joined_ref, padded, weighted,
):
    memory, norm, top, decay = block_state(
        base_ref, raw_ref, rim_ref, tap_ref, val_ref, rows_ref, cols_ref, act_ref, padded, weighted
    )
    write_record(rec_ref, memory, norm, top, decay)
    other_norm, other_top, other_decay = read_aux(other_ref[0, DK:ROWS])
    first = base_ref[1] == 0
    own_log = top + jnp.where(first, other_decay, 0.0)
    other_log = other_top + jnp.where(first, 0.0, decay)
    joined_top = jnp.maximum(own_log, other_log)
    own_weight = jnp.exp(own_log - joined_top)
    other_weight = jnp.exp(other_log - joined_top)
    aux = aux_rows(own_weight * norm + other_weight * other_norm, joined_top, decay + other_decay)
    for half in range(DV // HALF):
        own = memory[:, half * HALF : (half + 1) * HALF]
        joined_ref[half, 0:DK] = (own_weight * own + other_weight * other_ref[half, 0:DK].astype(F32)).astype(BF16)
        joined_ref[half, DK:ROWS] = aux


def state_call(base, raw, rim, taps, values, rows, cols, other=None):
    by_head = lambda n, width: pl.BlockSpec((n, width), lambda s, b: (0, b[0] + s))
    whole = lambda x: pl.BlockSpec(x.shape, lambda s, b: (0, 0))
    record = pl.BlockSpec((2, ROWS, HALF), lambda s, b: (s, 0, 0))
    in_specs = [by_head(BLK, DK), by_head(16, DK), by_head(TAPS, DK), by_head(BLK, DV), whole(rows), whole(cols)]
    out_specs = [record, pl.BlockSpec((BLK, DK), lambda s, b: (0, s))]
    record_shape = jax.ShapeDtypeStruct((2 * GROUP, ROWS, HALF), BF16)
    out_shape = [record_shape, jax.ShapeDtypeStruct((BLK, GROUP * DK), BF16)]
    operands = [raw, rim, taps, values, rows, cols]
    if other is not None:
        in_specs.append(record)
        out_specs.append(record)
        out_shape.append(record_shape)
        operands.append(other)
    return pl.pallas_call(
        send_kernel if other is None else pair_kernel,
        grid_spec=pltpu.PrefetchScalarGridSpec(
            num_scalar_prefetch=1,
            grid=(GROUP,),
            in_specs=in_specs,
            out_specs=out_specs,
            scratch_shapes=[pltpu.VMEM((BLK + 8, DK), F32), pltpu.VMEM((BLK, DK), BF16)],
        ),
        out_shape=out_shape,
        name="state_send" if other is None else "state_pair",
        cost_estimate=pl.CostEstimate(
            flops=GROUP * 2 * BLK * DK * DV, transcendentals=GROUP * BLK * DK, bytes_accessed=6 << 20
        ),
    )(base, *operands)


def near_kernel(base_ref, query_ref, key_ref, val_ref, rows_ref, cols_ref, prev_ref, num_ref, stat_ref):
    step = pl.program_id(0)
    head = base_ref[0] + step
    second = base_ref[1] == 1
    prev_aux = prev_ref[0, DK:ROWS]
    _, prev_top, prev_decay = read_aux(prev_aux)
    prev_top = jnp.where(second, prev_top, EMPTY)[:, 0:1]
    prev_decay = jnp.where(second, prev_decay, 0.0)[:, 0:1]
    peak = jnp.maximum(column(cols_ref, head), prev_top)
    prev_weight = jnp.where(second, jnp.exp(prev_top - peak), 0.0) * SCALE
    level = rows_ref[pl.ds(head, 1), :]
    causal = lax.broadcasted_iota(jnp.int32, (TILE, TILE), 0) >= lax.broadcasted_iota(
        jnp.int32, (TILE, TILE), 1
    )
    lanes = lax.broadcasted_iota(jnp.int32, (TILE, 128), 1)
    for t in range(0, BLK, TILE):
        query = query_ref[t : t + TILE]
        rows_peak = peak[t : t + TILE]
        den = jnp.zeros((TILE, 1), F32)
        num = None
        for s in range(0, t + TILE, TILE):
            scores = lax.dot_general(
                query, key_ref[s : s + TILE], (((1,), (1,)), ((), ())), preferred_element_type=F32
            )
            exponent = level[:, s : s + TILE] - rows_peak
            if s == t:
                exponent = jnp.where(causal, exponent, -jnp.inf)
            mixing = (scores * SCALE * jnp.exp(exponent)).astype(BF16)
            den = den + jnp.sum(mixing.astype(F32), axis=1, keepdims=True)
            part = jnp.dot(mixing, val_ref[s : s + TILE], preferred_element_type=F32)
            num = part if num is None else num + part
        weight = prev_weight[t : t + TILE]
        prev_den = lax.dot_general(query, prev_aux, (((1,), (1,)), ((), ())), preferred_element_type=F32)
        den = den + weight * (prev_den[:, 0:1] + prev_den[:, 1:2])
        for half in range(DV // HALF):
            lo, hi = half * HALF, (half + 1) * HALF
            far = jnp.dot(query, prev_ref[half, 0:DK], preferred_element_type=F32)
            num_ref[t : t + TILE, lo:hi] = num[:, lo:hi] + weight * far
        stat = jnp.where(step == 0, jnp.zeros((TILE, 128), F32), stat_ref[t : t + TILE])
        stat = jnp.where(lanes == step, den, stat)
        stat = jnp.where(lanes == GROUP + step, rows_peak, stat)
        stat = jnp.where(lanes == 2 * GROUP + step, prev_decay, stat)
        stat_ref[t : t + TILE] = stat


def near_call(base, query_act, key_act, values, rows, cols, prev):
    by_head = lambda width: pl.BlockSpec((BLK, width), lambda s, b: (0, b[0] + s))
    local = lambda width: pl.BlockSpec((BLK, width), lambda s, b: (0, s))
    whole = lambda shape: pl.BlockSpec(shape, lambda s, b: (0, 0))
    return pl.pallas_call(
        near_kernel,
        grid_spec=pltpu.PrefetchScalarGridSpec(
            num_scalar_prefetch=1,
            grid=(GROUP,),
            in_specs=[
                by_head(DK), local(DK), by_head(DV), whole(rows.shape), whole(cols.shape),
                pl.BlockSpec((2, ROWS, HALF), lambda s, b: (s, 0, 0)),
            ],
            out_specs=[local(DV), whole((BLK, 128))],
        ),
        out_shape=[
            jax.ShapeDtypeStruct((BLK, GROUP * DV), F32),
            jax.ShapeDtypeStruct((BLK, 128), F32),
        ],
        name="near",
        cost_estimate=pl.CostEstimate(
            flops=GROUP * 2 * BLK * BLK * (DK + DV), transcendentals=GROUP * BLK * BLK, bytes_accessed=9 << 20
        ),
    )(base, query_act, key_act, values, rows, cols, prev)


def total_kernel(valid_ref, rec_ref, out_ref):
    count = rec_ref.shape[0]
    norms, tops, decays = [], [], []
    for k in range(count):
        norm, top, decay = read_aux(rec_ref[k, DK:ROWS])
        norms.append(norm)
        tops.append(jnp.where(valid_ref[k] == 1, top, EMPTY))
        decays.append(decay)
    after = jnp.zeros((1, HALF), F32)
    logs = [None] * count
    for k in reversed(range(count)):
        logs[k] = tops[k] + after
        after = after + decays[k]
    peak = functools.reduce(jnp.maximum, logs)
    weights = [jnp.exp(log - peak) for log in logs]
    norm = sum(w * n for w, n in zip(weights, norms))
    for start in range(0, DK, STEP):
        acc = weights[0] * rec_ref[0, start : start + STEP].astype(F32)
        for k in range(1, count):
            acc = acc + weights[k] * rec_ref[k, start : start + STEP].astype(F32)
        out_ref[start : start + STEP] = acc.astype(BF16)
    out_ref[DK:ROWS] = aux_rows(norm, peak, after)


def total_call(valid, records):
    return pl.pallas_call(
        total_kernel,
        grid_spec=pltpu.PrefetchScalarGridSpec(
            num_scalar_prefetch=1,
            grid=(1,),
            in_specs=[pl.BlockSpec(records.shape, lambda s, v: (0, 0, 0))],
            out_specs=pl.BlockSpec((ROWS, HALF), lambda s, v: (0, 0)),
        ),
        out_shape=jax.ShapeDtypeStruct((ROWS, HALF), BF16),
        name="total",
    )(valid, records)


def prefix_kernel(valid_ref, rec_ref, enter_ref, out_ref):
    count = rec_ref.shape[0]
    norm, top, _ = read_aux(enter_ref[DK:ROWS])
    top = jnp.where(valid_ref[0] == 1, top, EMPTY)
    zero = jnp.zeros((1, HALF), F32)
    weights = []
    for k in range(count):
        out_ref[k, DK:ROWS] = aux_rows(norm, top, zero)
        if k + 1 < count:
            later_norm, later_top, decay = read_aux(rec_ref[k, DK:ROWS])
            joined = jnp.maximum(top + decay, later_top)
            early, late = jnp.exp(top + decay - joined), jnp.exp(later_top - joined)
            norm = early * norm + late * later_norm
            top = joined
            weights.append((early, late))
    for start in range(0, DK, STEP):
        run = enter_ref[start : start + STEP].astype(F32)
        for k in range(count):
            out_ref[k, start : start + STEP] = run.astype(BF16)
            if k + 1 < count:
                early, late = weights[k]
                run = early * run + late * rec_ref[k, start : start + STEP].astype(F32)


def prefix_call(valid, records, entering):
    return pl.pallas_call(
        prefix_kernel,
        grid_spec=pltpu.PrefetchScalarGridSpec(
            num_scalar_prefetch=1,
            grid=(1,),
            in_specs=[
                pl.BlockSpec(records.shape, lambda s, v: (0, 0, 0)),
                pl.BlockSpec((ROWS, HALF), lambda s, v: (0, 0)),
            ],
            out_specs=pl.BlockSpec(records.shape, lambda s, v: (0, 0, 0)),
        ),
        out_shape=jax.ShapeDtypeStruct(records.shape, BF16),
        name="prefix",
    )(valid, records, entering)


def far_kernel(base_ref, query_ref, num_ref, stat_ref, enter_ref, *refs):
    out_ref = refs[-1]
    step = pl.program_id(0)
    aux = enter_ref[0, DK:ROWS]
    _, top, _ = read_aux(aux)
    den = column(stat_ref, step)
    near_peak = column(stat_ref, GROUP + step)
    far_log = top[:, 0:1] + column(stat_ref, 2 * GROUP + step)
    peak = jnp.maximum(near_peak, far_log)
    near_weight = jnp.exp(near_peak - peak)
    far_weight = jnp.exp(far_log - peak) * SCALE
    for t in range(0, BLK, TILE):
        query = query_ref[t : t + TILE]
        near_part = near_weight[t : t + TILE]
        far_part = far_weight[t : t + TILE]
        far_den = lax.dot_general(query, aux, (((1,), (1,)), ((), ())), preferred_element_type=F32)
        below = near_part * den[t : t + TILE] + far_part * (far_den[:, 0:1] + far_den[:, 1:2])
        scale = 1.0 / jnp.maximum(jnp.abs(below), 1.0)
        near_part = near_part * scale
        far_part = far_part * scale
        for half in range(DV // HALF):
            lo, hi = half * HALF, (half + 1) * HALF
            far = jnp.dot(query, enter_ref[half, 0:DK], preferred_element_type=F32)
            out_ref[t : t + TILE, lo:hi] = (near_part * num_ref[t : t + TILE, lo:hi] + far_part * far).astype(BF16)


def far_call(base, query_act, num, stat, entering, out=None):
    by_head = lambda width: pl.BlockSpec((BLK, width), lambda s, b: (0, b[0] + s))
    in_specs = [
        by_head(DK),
        pl.BlockSpec((BLK, DV), lambda s, b: (0, s)),
        pl.BlockSpec((BLK, 128), lambda s, b: (0, 0)),
        pl.BlockSpec((2, ROWS, HALF), lambda s, b: (s, 0, 0)),
    ]
    operands = [query_act, num, stat, entering]
    aliases = {}
    if out is not None:
        in_specs.append(pl.BlockSpec(memory_space=pl.ANY))
        operands.append(out)
        aliases = {len(operands): 0}
    return pl.pallas_call(
        far_kernel,
        grid_spec=pltpu.PrefetchScalarGridSpec(
            num_scalar_prefetch=1, grid=(GROUP,), in_specs=in_specs, out_specs=by_head(DV)
        ),
        out_shape=jax.ShapeDtypeStruct((BLK, HEADS * DV), BF16),
        input_output_aliases=aliases,
        name="far",
        cost_estimate=pl.CostEstimate(
            flops=GROUP * 2 * BLK * DK * DV, transcendentals=0, bytes_accessed=9 << 20
        ),
    )(base, *operands)


def on_device(query_raw, key_raw, values, in_gate, forget_gate, query_conv, key_conv):
    devices = lax.axis_size(AXES)
    me = lax.axis_index(AXES)
    core = me % 2
    cube_size = 2 * 2 * GROUP
    cubes = devices // cube_size
    cube = me // cube_size
    base_mine = jnp.stack([GROUP * core, core]).astype(jnp.int32)
    base_theirs = jnp.stack([GROUP * (1 - core), core]).astype(jnp.int32)
    line = [(i, i + 1) for i in range(devices - 1)]
    swap = [(i, i ^ 1) for i in range(devices)]
    forward = [(i, i + 1) for i in range(0, devices, 2)]
    owners = [
        [g * cube_size + 2 * k + c for k in range(2 * GROUP)] for g in range(cubes) for c in range(2)
    ]

    rim = lax.ppermute(jnp.concatenate([key_raw[-16:], query_raw[-16:]], axis=1), AXES, line)
    width = key_raw.shape[1]
    rim_key, rim_query = rim[:, :width], rim[:, width:]
    rows, cols = gates(in_gate, forget_gate)

    sent, key_theirs = state_call(base_theirs, key_raw, rim_key, key_conv, values, rows, cols)
    other_mine = lax.ppermute(sent, AXES, swap)
    query_act = query_conv_act(query_raw, rim_query, query_conv)
    own, key_mine, joined = state_call(base_mine, key_raw, rim_key, key_conv, values, rows, cols, other_mine)

    pieces = lax.all_to_all(joined, AXES, 0, 0, axis_index_groups=owners, tiled=True)
    other_theirs = lax.ppermute(own, AXES, forward)
    num_mine, stat_mine = near_call(base_mine, query_act, key_mine, values, rows, cols, other_mine)
    num_theirs, stat_theirs = near_call(base_theirs, query_act, key_theirs, values, rows, cols, other_theirs)

    total = total_call(jnp.ones((2 * GROUP,), jnp.int32), pieces)
    up = lambda distance: [(i, i + distance * cube_size) for i in range(devices - distance * cube_size)]
    entering = lax.ppermute(total, AXES, up(1))
    distance = 1
    while distance < cubes - 1:
        earlier = lax.ppermute(entering, AXES, up(distance))
        valid = jnp.stack([cube > distance, cube > 0]).astype(jnp.int32)
        entering = total_call(valid, jnp.stack([earlier, entering]))
        distance *= 2
    before = prefix_call((cube > 0).astype(jnp.int32)[None], pieces, entering)
    enter_mine = lax.all_to_all(before, AXES, 0, 0, axis_index_groups=owners, tiled=True)
    enter_theirs = lax.ppermute(enter_mine, AXES, swap)

    out = far_call(base_mine, query_act, num_mine, stat_mine, enter_mine)
    return far_call(base_theirs, query_act, num_theirs, stat_theirs, enter_theirs, out)


def solution(mesh):
    split = P(AXES, None)
    in_specs = (split, split, split, split, split, P(), P())
    return jax.shard_map(on_device, mesh=mesh, in_specs=in_specs, out_specs=split, check_vma=False)
```

```python
import functools

import jax
import jax.numpy as jnp
from jax import lax
from jax.experimental import pallas as pl
from jax.experimental.pallas import tpu as pltpu
from jax.sharding import PartitionSpec as P

AXES = ("ctx", "head")
HEADS = 8
CHAINS = 1
GROUP = HEADS // 2
LOCAL = GROUP // CHAINS
OWNERS = 8
DK = 256
DV = 512
WIDTH = LOCAL * DV // OWNERS
PIECES = DV // WIDTH
SPLIT = DK // WIDTH
AUX = 16
ROWS = DK + AUX
BLK = 512
TAPS = 4
TILE = 256
STEP = 128
EMPTY = -1e30
SCALE = DK**-0.5
F32 = jnp.float32
BF16 = jnp.bfloat16
NUM = BF16
NT = (((1,), (1,)), ((), ()))


def narrow(x):
    return x.astype(BF16).astype(F32)


def split3(x):
    top = narrow(x)
    middle = narrow(x - top)
    return [top, middle, x - top - middle]


def aux_rows(norms, top, decay):
    parts = []
    for norm in norms:
        high = narrow(norm)
        parts += [high, norm - high]
    parts += split3(top) + split3(decay)
    row = lax.broadcasted_iota(jnp.int32, (AUX, WIDTH), 0)
    out = jnp.zeros((AUX, WIDTH), F32)
    for index, part in enumerate(parts):
        out = jnp.where(row == index, part, out)
    return out.astype(BF16)


def read_aux(aux):
    aux = aux.astype(F32)
    norms = [aux[2 * k : 2 * k + 1] + aux[2 * k + 1 : 2 * k + 2] for k in range(SPLIT)]
    at = 2 * SPLIT
    top = aux[at : at + 1] + aux[at + 1 : at + 2] + aux[at + 2 : at + 3]
    decay = aux[at + 3 : at + 4] + aux[at + 4 : at + 5] + aux[at + 5 : at + 6]
    return norms, top, decay


def dot_norm(aux, query):
    out = None
    for k in range(SPLIT):
        part = lax.dot_general(
            aux, query[:, k * WIDTH : (k + 1) * WIDTH], NT, preferred_element_type=F32
        )
        part = part[2 * k : 2 * k + 1] + part[2 * k + 1 : 2 * k + 2]
        out = part if out is None else out + part
    return out


def column(row):
    return jnp.broadcast_to(row, (128, row.shape[1])).T


def widen(col, width):
    return jnp.concatenate([col] * (width // 128), axis=1)


def place():
    me = lax.axis_index("ctx") * lax.axis_size("head") + lax.axis_index("head")
    return me % 2, me // (2 * OWNERS)


def first_head(mine, chain):
    core, _ = place()
    return GROUP * (core if mine else 1 - core) + LOCAL * chain


def span(index, width):
    return pl.ds(pl.multiple_of(index * width, width), width)


VMEM_SPEC = pl.BlockSpec(memory_space=pltpu.VMEM)


def on_chip(kernel, operands, shapes, scratch=(), name=None, flops=0, size=1 << 20):
    many = isinstance(shapes, list)
    kept = [pltpu.with_memory_space_constraint(x, pltpu.VMEM) for x in operands]
    out = [pltpu.VMEM(shape, dtype) for shape, dtype in (shapes if many else [shapes])]
    results = pl.pallas_call(
        kernel,
        in_specs=[VMEM_SPEC] * len(kept),
        out_specs=[VMEM_SPEC] * len(out),
        out_shape=out,
        scratch_shapes=list(scratch),
        name=name,
        cost_estimate=pl.CostEstimate(flops=flops, transcendentals=0, bytes_accessed=size),
        compiler_params=pltpu.CompilerParams(vmem_limit_bytes=8 << 20),
    )(*kept)
    return results if many else results[0]


def tails_kernel(key_hbm, query_hbm, out_ref, sems):
    width = key_hbm.shape[1]
    last = pl.ds(BLK - AUX, AUX)
    for copy in start_all(
        [
            pltpu.make_async_copy(key_hbm.at[last], out_ref.at[:, 0:width], sems.at[0]),
            pltpu.make_async_copy(query_hbm.at[last], out_ref.at[:, width : 2 * width], sems.at[1]),
        ]
    ):
        copy.wait()


def tails_call(key_raw, query_raw):
    return kernel_call(
        tails_kernel,
        [("hbm", key_raw), ("hbm", query_raw)],
        [("vmem", (AUX, 2 * key_raw.shape[1]), BF16)],
        [pltpu.SemaphoreType.DMA((2,))],
        "tails",
        0,
        1 << 17,
    )[0]


def prepare_kernel(in_hbm, forget_hbm, key_hbm, tap_hbm, val_hbm, rows_ref, key_ref, tap_ref, val_ref, gate_buf, sems):
    gates_in = start_all(
        [
            pltpu.make_async_copy(in_hbm, gate_buf.at[0], sems.at[0]),
            pltpu.make_async_copy(forget_hbm, gate_buf.at[1], sems.at[1]),
        ]
    )
    loads = start_all(
        [
            pltpu.make_async_copy(key_hbm, key_ref, sems.at[2]),
            pltpu.make_async_copy(tap_hbm, tap_ref, sems.at[3]),
            pltpu.make_async_copy(val_hbm, val_ref, sems.at[4]),
        ]
    )
    for copy in gates_in:
        copy.wait()
    gate = gate_buf[0].astype(F32)
    forget = gate_buf[1].astype(F32)
    log_forget = jnp.minimum(forget, 0.0) - jnp.log1p(jnp.exp(-jnp.abs(forget)))
    lane = lax.broadcasted_iota(jnp.int32, (HEADS, BLK), 1)
    total = log_forget
    shift = 1
    while shift < BLK:
        total = total + jnp.where(lane >= shift, pltpu.roll(total, shift, 1), 0.0)
        shift *= 2
    level = gate - total
    top = level
    shift = 1
    while shift < BLK:
        top = jnp.maximum(top, jnp.where(lane >= shift, pltpu.roll(top, shift, 1), -jnp.inf))
        shift *= 2
    last_top = top[:, BLK - 1 :]
    last_total = total[:, BLK - 1 :]
    out = (
        level,
        top,
        jnp.exp(level - last_top),
        jnp.broadcast_to(last_total + last_top, (HEADS, BLK)),
        jnp.broadcast_to(last_total, (HEADS, BLK)),
    )
    for index, part in enumerate(out):
        rows_ref[index * HEADS : (index + 1) * HEADS] = part
    for copy in loads:
        copy.wait()


def prepare_call(in_gate, forget_gate, key_raw, key_conv, values):
    return kernel_call(
        prepare_kernel,
        [("hbm", in_gate.T), ("hbm", forget_gate.T), ("hbm", key_raw), ("hbm", key_conv), ("hbm", values)],
        [
            ("vmem", (5 * HEADS, BLK), F32),
            ("vmem", key_raw.shape, BF16),
            ("vmem", key_conv.shape, BF16),
            ("vmem", values.shape, BF16),
        ],
        [pltpu.VMEM((2, HEADS, BLK), BF16), pltpu.SemaphoreType.DMA((5,))],
        "prepare",
        0,
        6 << 20,
    )


def row_of(rows_ref, kind, head):
    return rows_ref[pl.ds(kind * HEADS + head, 1), :]


PADDED = pltpu.VMEM((BLK + 8, DK), F32)
HBM_SPEC = pl.BlockSpec(memory_space=pltpu.HBM)
LIMIT = 20 << 20


def kernel_call(kernel, inputs, outputs, scratch, name, flops, size):
    in_specs, operands = [], []
    for where, x in inputs:
        operands.append(pltpu.with_memory_space_constraint(x, pltpu.VMEM if where == "vmem" else pltpu.HBM))
        in_specs.append(VMEM_SPEC if where == "vmem" else HBM_SPEC)
    return pl.pallas_call(
        kernel,
        in_specs=in_specs,
        out_specs=[VMEM_SPEC if where == "vmem" else HBM_SPEC for where, _, _ in outputs],
        out_shape=[
            (pltpu.VMEM if where == "vmem" else pltpu.HBM)(shape, dtype)
            for where, shape, dtype in outputs
        ],
        scratch_shapes=scratch,
        name=name,
        cost_estimate=pl.CostEstimate(flops=flops, transcendentals=0, bytes_accessed=size),
        compiler_params=pltpu.CompilerParams(vmem_limit_bytes=LIMIT),
    )(*operands)


def conv_rows(columns, rim_columns, raw, rim_ref, tap_ref, padded):
    padded[0:8] = rim_ref[:, rim_columns].astype(F32)[8:16]
    padded[8 : 8 + BLK] = raw.astype(F32)
    taps = tap_ref[:, columns].astype(F32)
    for start in range(0, BLK, STEP):
        first = 8 - (TAPS - 1) + start
        mixed = taps[0:1] * padded[first : first + STEP]
        for tap in range(1, TAPS):
            mixed = mixed + taps[tap : tap + 1] * padded[first + tap : first + tap + STEP]
        yield start, (mixed * (0.5 * jnp.tanh(0.5 * mixed) + 0.5)).astype(BF16)


def start_all(copies):
    for copy in copies:
        copy.start()
    return copies


def state_kernel(mine, chain, raw_ref, rim_ref, tap_ref, val_ref, rows_ref, rec_ref, act_hbm, act_buf, padded, weighted, sems):
    head0 = first_head(mine, chain)
    act_out = []
    for local in range(LOCAL):
        head = head0 + local
        weight = column(row_of(rows_ref, 2, head))
        norm = jnp.zeros((1, DK), F32)
        columns = span(head, DK)
        for start, act in conv_rows(columns, columns, raw_ref[:, columns], rim_ref, tap_ref, padded.at[local % 2]):
            act_buf[local, start : start + STEP] = act
            scaled = act.astype(F32) * widen(weight[start : start + STEP], DK)
            norm = norm + jnp.sum(scaled, axis=0, keepdims=True)
            weighted[local % 2, start : start + STEP] = scaled.astype(BF16)
        act_out.append(
            pltpu.make_async_copy(act_buf.at[local], act_hbm.at[:, local * DK : (local + 1) * DK], sems.at[local])
        )
        act_out[-1].start()
        memory = lax.dot_general(
            weighted[local % 2], val_ref[:, span(head, DV)], (((0,), (0,)), ((), ())), preferred_element_type=F32
        )
        top = row_of(rows_ref, 3, head)[:, :WIDTH]
        decay = row_of(rows_ref, 4, head)[:, :WIDTH]
        aux = aux_rows([norm[:, k * WIDTH : (k + 1) * WIDTH] for k in range(SPLIT)], top, decay)
        for piece in range(PIECES):
            at = local * PIECES + piece
            rec_ref[at, 0:DK] = memory[:, piece * WIDTH : (piece + 1) * WIDTH].astype(BF16)
            rec_ref[at, DK:ROWS] = aux
    for copy in act_out:
        copy.wait()


def state_call(mine, chain, raw, rim, taps, values, rows):
    return kernel_call(
        functools.partial(state_kernel, mine, chain),
        [("vmem", raw), ("vmem", rim), ("vmem", taps), ("vmem", values), ("vmem", rows)],
        [("vmem", (OWNERS, ROWS, WIDTH), BF16), ("hbm", (BLK, LOCAL * DK), BF16)],
        [
            pltpu.VMEM((LOCAL, BLK, DK), BF16),
            pltpu.VMEM((2, BLK + 8, DK), F32),
            pltpu.VMEM((2, BLK, DK), BF16),
            pltpu.SemaphoreType.DMA((LOCAL,)),
        ],
        "state",
        LOCAL * 2 * BLK * DK * DV,
        LOCAL * 3 << 20,
    )


def merge(early, late):
    norms, top, decay = early
    later_norms, later_top, later_decay = late
    joined_top = jnp.maximum(top + later_decay, later_top)
    before = jnp.exp(top + later_decay - joined_top)
    after = jnp.exp(later_top - joined_top)
    joined = [before * a + after * b for a, b in zip(norms, later_norms)]
    return before, after, (joined, joined_top, decay + later_decay)


def join_kernel(own_ref, other_ref, out_hbm, first_hbm, out_buf, sems):
    second = place()[0] == 1
    held = pltpu.make_async_copy(own_ref, first_hbm, sems.at[LOCAL])
    passed = pltpu.make_async_copy(other_ref, first_hbm, sems.at[LOCAL])

    @pl.when(second)
    def _():
        passed.start()

    @pl.when(jnp.logical_not(second))
    def _():
        held.start()

    copies = []
    for local in range(LOCAL):
        at = local * PIECES
        norms, top, decay = read_aux(own_ref[at, DK:ROWS])
        other_norms, other_top, other_decay = read_aux(other_ref[at, DK:ROWS])
        own_log = top + jnp.where(second, 0.0, other_decay)
        other_log = other_top + jnp.where(second, decay, 0.0)
        joined_top = jnp.maximum(own_log, other_log)
        own_weight = jnp.exp(own_log - joined_top)
        other_weight = jnp.exp(other_log - joined_top)
        joined = [own_weight * a + other_weight * b for a, b in zip(norms, other_norms)]
        aux = aux_rows(joined, joined_top, decay + other_decay)
        for piece in range(PIECES):
            own = own_ref[at + piece, 0:DK].astype(F32)
            other = other_ref[at + piece, 0:DK].astype(F32)
            out_buf[at + piece, 0:DK] = (own_weight * own + other_weight * other).astype(BF16)
            out_buf[at + piece, DK:ROWS] = aux
        part = pl.ds(at, PIECES)
        copies.append(pltpu.make_async_copy(out_buf.at[part], out_hbm.at[part], sems.at[local]))
        copies[-1].start()
    for copy in copies:
        copy.wait()
    held.wait()


def join_call(own, other):
    return kernel_call(
        join_kernel,
        [("vmem", own), ("vmem", other)],
        [("hbm", own.shape, BF16)] * 2,
        [pltpu.VMEM(own.shape, BF16), pltpu.SemaphoreType.DMA((LOCAL + 1,))],
        "join",
        0,
        4 << 20,
    )


def split_kernel(enter_ref, first_ref, keep_ref, send_ref):
    second = place()[0] == 1
    for local in range(LOCAL):
        at = local * PIECES
        early = read_aux(enter_ref[at, DK:ROWS])
        before, after, joined = merge(early, read_aux(first_ref[at, DK:ROWS]))
        aux = aux_rows(*joined)
        plain = enter_ref[at, DK:ROWS]
        for piece in range(PIECES):
            chip = enter_ref[at + piece, 0:DK]
            moved = before * chip.astype(F32) + after * first_ref[at + piece, 0:DK].astype(F32)
            moved = moved.astype(BF16)
            keep_ref[at + piece, 0:DK] = jnp.where(second, moved, chip)
            send_ref[at + piece, 0:DK] = jnp.where(second, chip, moved)
            keep_ref[at + piece, DK:ROWS] = jnp.where(second, aux, plain)
            send_ref[at + piece, DK:ROWS] = jnp.where(second, plain, aux)


def split_call(enter, first):
    return kernel_call(
        split_kernel,
        [("vmem", enter), ("vmem", first)],
        [("vmem", enter.shape, BF16)] * 2,
        [],
        "split",
        0,
        4 << 20,
    )


def near_kernel(
    mine, chain, raw_hbm, rim_ref, tap_hbm, key_hbm, val_hbm, rows_ref,
    query_hbm, num_hbm, stat_ref,
    raw_buf, key_buf, val_buf, query_buf, num_buf, tap_buf, padded, sems,
):
    head0 = first_head(mine, chain)
    taps_in = pltpu.make_async_copy(tap_hbm, tap_buf, sems.at[5 * LOCAL])
    taps_in.start()
    coming, going = [], []
    for local in range(LOCAL):
        mid, wide = slice(local * DK, (local + 1) * DK), slice(local * DV, (local + 1) * DV)
        pairs = (
            (raw_hbm.at[:, span(head0 + local, DK)], raw_buf.at[local]),
            (key_hbm.at[:, mid], key_buf.at[local]),
            (val_hbm.at[:, span(head0 + local, DV)], val_buf.at[local]),
            (query_buf.at[local], query_hbm.at[:, mid]),
            (num_buf.at[local], num_hbm.at[:, wide]),
        )
        copies = [pltpu.make_async_copy(a, b, sems.at[5 * local + k]) for k, (a, b) in enumerate(pairs)]
        coming.append(start_all(copies[:3]))
        going.append(copies[3:])
    taps_in.wait()
    causal = lax.broadcasted_iota(jnp.int32, (TILE, TILE), 0) >= lax.broadcasted_iota(
        jnp.int32, (TILE, TILE), 1
    )
    ones = jnp.ones((8, TILE), BF16)
    for local in range(LOCAL):
        head = head0 + local
        coming[local][0].wait()
        columns, rim_columns = span(head, DK), span(HEADS + head, DK)
        for start, act in conv_rows(columns, rim_columns, raw_buf[local], rim_ref, tap_buf, padded.at[local % 2]):
            query_buf[local, start : start + STEP] = act
        going[local][0].start()
        coming[local][1].wait()
        coming[local][2].wait()
        peak = row_of(rows_ref, 1, head)
        level = row_of(rows_ref, 0, head)
        peak_column = column(peak)
        for t in range(0, BLK, TILE):
            query = query_buf[local, t : t + TILE]
            rows_peak = widen(peak_column[t : t + TILE], TILE)
            den = jnp.zeros((1, TILE), F32)
            num = None
            for s in range(0, t + TILE, TILE):
                scores = lax.dot_general(query, key_buf[local, s : s + TILE], NT, preferred_element_type=F32)
                exponent = level[:, s : s + TILE] - rows_peak
                if s == t:
                    exponent = jnp.where(causal, exponent, -jnp.inf)
                mixing = (scores * (SCALE * jnp.exp(exponent))).astype(BF16)
                den = den + lax.dot_general(ones, mixing, NT, preferred_element_type=F32)[0:1]
                part = jnp.dot(mixing, val_buf[local, s : s + TILE], preferred_element_type=F32)
                num = part if num is None else num + part
            num_buf[local, t : t + TILE] = num.astype(NUM)
            stat_ref[local, 0:1, t : t + TILE] = den
        going[local][1].start()
        stat_ref[local, 1:2] = peak
        stat_ref[local, 2:8] = jnp.zeros((6, BLK), F32)
    for copies in going:
        for copy in copies:
            copy.wait()


def near_call(mine, chain, raw, rim, taps, key_act, values, rows):
    return kernel_call(
        functools.partial(near_kernel, mine, chain),
        [("hbm", raw), ("vmem", rim), ("hbm", taps), ("hbm", key_act), ("hbm", values), ("vmem", rows)],
        [
            ("hbm", (BLK, LOCAL * DK), BF16),
            ("hbm", (BLK, LOCAL * DV), NUM),
            ("vmem", (LOCAL, 8, BLK), F32),
        ],
        [
            pltpu.VMEM((LOCAL, BLK, DK), BF16),
            pltpu.VMEM((LOCAL, BLK, DK), BF16),
            pltpu.VMEM((LOCAL, BLK, DV), BF16),
            pltpu.VMEM((LOCAL, BLK, DK), BF16),
            pltpu.VMEM((LOCAL, BLK, DV), NUM),
            pltpu.VMEM((TAPS, HEADS * DK), BF16),
            pltpu.VMEM((2, BLK + 8, DK), F32),
            pltpu.SemaphoreType.DMA((5 * LOCAL + 1,)),
        ],
        "near",
        LOCAL * 2 * BLK * BLK * (DK + DV),
        LOCAL * 5 << 20,
    )


def total_kernel(rule, rec_ref, out_ref):
    count = rec_ref.shape[0]
    norms, tops, decays = [], [], []
    for k in range(count):
        norm, top, decay = read_aux(rec_ref[k, DK:ROWS])
        norms.append(norm)
        tops.append(top if rule is None else jnp.where(place()[1] > rule[k], top, EMPTY))
        decays.append(decay)
    after = jnp.zeros((1, WIDTH), F32)
    logs = [None] * count
    for k in reversed(range(count)):
        logs[k] = tops[k] + after
        after = after + decays[k]
    peak = functools.reduce(jnp.maximum, logs)
    weights = [jnp.exp(log - peak) for log in logs]
    joined = [sum(w * n[part] for w, n in zip(weights, norms)) for part in range(SPLIT)]
    for start in range(0, DK, STEP):
        acc = weights[0] * rec_ref[0, start : start + STEP].astype(F32)
        for k in range(1, count):
            acc = acc + weights[k] * rec_ref[k, start : start + STEP].astype(F32)
        out_ref[start : start + STEP] = acc.astype(BF16)
    out_ref[DK:ROWS] = aux_rows(joined, peak, after)


def total_call(records, rule=None):
    return on_chip(functools.partial(total_kernel, rule), [records], ((ROWS, WIDTH), BF16), name="total")


def prefix_kernel(rec_ref, enter_ref, out_hbm, out_buf, sems):
    count = rec_ref.shape[0]
    norms, top, _ = read_aux(enter_ref[DK:ROWS])
    state = (norms, jnp.where(place()[1] > 0, top, EMPTY), jnp.zeros((1, WIDTH), F32))
    weights = []
    for k in range(count):
        out_buf[k, DK:ROWS] = aux_rows(*state)
        if k + 1 < count:
            early, late, state = merge(state, read_aux(rec_ref[k, DK:ROWS]))
            weights.append((early, late))
    for start in range(0, DK, STEP):
        run = enter_ref[start : start + STEP].astype(F32)
        for k in range(count):
            out_buf[k, start : start + STEP] = run.astype(BF16)
            if k + 1 < count:
                early, late = weights[k]
                run = early * run + late * rec_ref[k, start : start + STEP].astype(F32)
    copy = pltpu.make_async_copy(out_buf, out_hbm, sems.at[0])
    copy.start()
    copy.wait()


def prefix_call(records, entering):
    return kernel_call(
        prefix_kernel,
        [("vmem", records), ("vmem", entering)],
        [("hbm", records.shape, BF16)],
        [pltpu.VMEM(records.shape, BF16), pltpu.SemaphoreType.DMA((1,))],
        "prefix",
        0,
        2 << 20,
    )[0]


def far_kernel(mine, chain, query_ref, num_ref, stat_ref, enter_ref, *refs):
    out_ref, ready, sems = refs[-3:]
    copies = []
    for local in range(LOCAL):
        mid, wide = slice(local * DK, (local + 1) * DK), slice(local * DV, (local + 1) * DV)
        at = local * PIECES
        aux = enter_ref[at, DK:ROWS]
        _, top, _ = read_aux(aux)
        query = query_ref[:, mid]
        den = stat_ref[local, 0:1]
        near_peak = stat_ref[local, 1:2]
        far_log = top[:, 0:1]
        peak = jnp.maximum(near_peak, far_log)
        near_part = jnp.exp(near_peak - peak)
        far_part = jnp.exp(far_log - peak) * SCALE
        below = near_part * den + far_part * dot_norm(aux, query)
        scale = 1.0 / jnp.maximum(jnp.abs(below), 1.0)
        near_column = column(near_part * scale)
        far_column = column(far_part * scale)
        memory = jnp.concatenate([enter_ref[at + piece, 0:DK] for piece in range(PIECES)], axis=1)
        for t in range(0, BLK, STEP):
            far = jnp.dot(query[t : t + STEP], memory, preferred_element_type=F32)
            near_weight = widen(near_column[t : t + STEP], DV)
            far_weight = widen(far_column[t : t + STEP], DV)
            ready[local, t : t + STEP] = (near_weight * num_ref[t : t + STEP, wide].astype(F32) + far_weight * far).astype(BF16)
        head = first_head(mine, chain) + local
        copies.append(pltpu.make_async_copy(ready.at[local], out_ref.at[:, span(head, DV)], sems.at[local]))
        copies[-1].start()
    for copy in copies:
        copy.wait()


def far_call(mine, chain, query_act, num, stat, entering, out=None):
    operands = [pltpu.with_memory_space_constraint(x, pltpu.VMEM) for x in (query_act, num, stat, entering)]
    in_specs = [VMEM_SPEC] * len(operands)
    aliases = {}
    if out is not None:
        in_specs.append(pl.BlockSpec(memory_space=pltpu.HBM))
        aliases = {len(operands): 0}
        operands.append(out)
    return pl.pallas_call(
        functools.partial(far_kernel, mine, chain),
        in_specs=in_specs,
        out_specs=pl.BlockSpec(memory_space=pltpu.HBM),
        out_shape=jax.ShapeDtypeStruct((BLK, HEADS * DV), BF16),
        scratch_shapes=[pltpu.VMEM((LOCAL, BLK, DV), BF16), pltpu.SemaphoreType.DMA((LOCAL,))],
        input_output_aliases=aliases,
        compiler_params=pltpu.CompilerParams(vmem_limit_bytes=8 << 20),
        name="far",
        cost_estimate=pl.CostEstimate(
            flops=LOCAL * 2 * BLK * DK * DV, transcendentals=0, bytes_accessed=LOCAL * 5 << 20
        ),
    )(*operands)


def on_device(query_raw, key_raw, values, in_gate, forget_gate, query_conv, key_conv):
    devices = lax.axis_size(AXES)
    cube_size = 2 * OWNERS
    cubes = devices // cube_size
    line = [(i, i + 1) for i in range(devices - 1)]
    swap = [(i, i ^ 1) for i in range(devices)]
    forward = [(i, i + 1) for i in range(0, devices, 2)]
    owners = [
        [g * cube_size + 2 * k + c for k in range(OWNERS)] for g in range(cubes) for c in range(2)
    ]
    up = lambda distance: [(i, i + distance * cube_size) for i in range(devices - distance * cube_size)]
    spread = lambda x: lax.all_to_all(x, AXES, 0, 0, axis_index_groups=owners, tiled=True)
    after = lambda x, *done: lax.optimization_barrier((x,) + done)[0]

    chains = range(CHAINS)
    key_mine, key_theirs, other_mine, first = ([None] * CHAINS for _ in range(4))
    pieces, entering, enter_mine, enter_theirs = ([None] * CHAINS for _ in range(4))
    near_mine, near_theirs = ([None] * CHAINS for _ in range(2))

    rim = lax.ppermute(tails_call(key_raw, query_raw), AXES, line)
    rows, key_held, taps_held, val_held = prepare_call(in_gate, forget_gate, key_raw, key_conv, values)

    for c in chains:
        sent, key_theirs[c] = state_call(False, c, key_held, rim, taps_held, val_held, rows)
        rows = after(rows, sent)
        other_mine[c] = lax.ppermute(sent, AXES, swap)
    for c in chains:
        own, key_mine[c] = state_call(True, c, key_held, rim, taps_held, val_held, rows)
        joined, first[c] = join_call(own, other_mine[c])
        rows = after(rows, joined)
        pieces[c] = spread(joined)
    for c in chains:
        near_mine[c] = near_call(True, c, query_raw, rim, query_conv, key_mine[c], values, rows)
        rows = after(rows, near_mine[c][0])
        near_theirs[c] = near_call(False, c, query_raw, rim, query_conv, key_theirs[c], values, rows)
        pieces[c] = after(pieces[c], near_theirs[c][0])
        total = total_call(pieces[c])
        rows = after(rows, total)
        entering[c] = lax.ppermute(total, AXES, up(1))
        distance = 1
        while distance < cubes - 1:
            earlier = lax.ppermute(entering[c], AXES, up(distance))
            entering[c] = total_call(jnp.stack([earlier, entering[c]]), (distance, 0))
            distance *= 2
    for c in chains:
        before = prefix_call(pieces[c], entering[c])
        rows = after(rows, before)
        enter_mine[c] = spread(before)
    out = None
    for c in chains:
        keep, send = split_call(enter_mine[c], first[c])
        enter_theirs[c] = lax.ppermute(send, AXES, swap)
        out = far_call(True, c, *near_mine[c], keep, out)
        out = far_call(False, c, *near_theirs[c], enter_theirs[c], out)
    return out


def solution(mesh):
    split = P(AXES, None)
    in_specs = (split, split, split, split, split, P(), P())
    return jax.shard_map(on_device, mesh=mesh, in_specs=in_specs, out_specs=split, check_vma=False)
```

```python
import functools

import jax
import jax.numpy as jnp
from jax import lax
from jax.experimental import pallas as pl
from jax.experimental.pallas import tpu as pltpu
from jax.sharding import PartitionSpec as P

AXES = ("ctx", "head")
HEADS = 8
CHAINS = 1
GROUP = HEADS // 2
LOCAL = GROUP // CHAINS
OWNERS = 8
DK = 256
DV = 512
WIDTH = LOCAL * DV // OWNERS
PIECES = DV // WIDTH
SPLIT = DK // WIDTH
AUX = 16
ROWS = DK + AUX
BLK = 512
TAPS = 4
TILE = 256
STEP = 128
EMPTY = -1e30
ORDER = (7, 6, 5, 3, 4, 2, 1)
SIDES = [(True, local) for local in range(LOCAL)] + [(False, local) for local in range(LOCAL)]
PARTS = (SIDES[:4], SIDES[4:6], SIDES[6:])
SCALE = DK**-0.5
F32 = jnp.float32
BF16 = jnp.bfloat16
NUM = BF16
NT = (((1,), (1,)), ((), ()))


def narrow(x):
    return x.astype(BF16).astype(F32)


def split3(x):
    top = narrow(x)
    middle = narrow(x - top)
    return [top, middle, x - top - middle]


def aux_rows(norms, top, decay):
    parts = []
    for norm in norms:
        high = narrow(norm)
        parts += [high, norm - high]
    parts += split3(top) + split3(decay)
    row = lax.broadcasted_iota(jnp.int32, (AUX, WIDTH), 0)
    out = jnp.zeros((AUX, WIDTH), F32)
    for index, part in enumerate(parts):
        out = jnp.where(row == index, part, out)
    return out.astype(BF16)


def read_aux(aux):
    aux = aux.astype(F32)
    norms = [aux[2 * k : 2 * k + 1] + aux[2 * k + 1 : 2 * k + 2] for k in range(SPLIT)]
    at = 2 * SPLIT
    top = aux[at : at + 1] + aux[at + 1 : at + 2] + aux[at + 2 : at + 3]
    decay = aux[at + 3 : at + 4] + aux[at + 4 : at + 5] + aux[at + 5 : at + 6]
    return norms, top, decay


def dot_norm(aux, query):
    out = None
    for k in range(SPLIT):
        part = lax.dot_general(
            aux, query[:, k * WIDTH : (k + 1) * WIDTH], NT, preferred_element_type=F32
        )
        part = part[2 * k : 2 * k + 1] + part[2 * k + 1 : 2 * k + 2]
        out = part if out is None else out + part
    return out


def column(row):
    return jnp.broadcast_to(row, (128, row.shape[1])).T


def widen(col, width):
    return jnp.concatenate([col] * (width // 128), axis=1)


def place():
    me = lax.axis_index("ctx") * lax.axis_size("head") + lax.axis_index("head")
    return me % 2, me // (2 * OWNERS), me % (2 * OWNERS) // 2


def first_head(mine, chain):
    core = place()[0]
    return GROUP * (core if mine else 1 - core) + LOCAL * chain


def span(index, width):
    return pl.ds(pl.multiple_of(index * width, width), width)


VMEM_SPEC = pl.BlockSpec(memory_space=pltpu.VMEM)


def on_chip(kernel, operands, shapes, scratch=(), name=None, flops=0, size=1 << 20):
    many = isinstance(shapes, list)
    kept = [pltpu.with_memory_space_constraint(x, pltpu.VMEM) for x in operands]
    out = [pltpu.VMEM(shape, dtype) for shape, dtype in (shapes if many else [shapes])]
    results = pl.pallas_call(
        kernel,
        in_specs=[VMEM_SPEC] * len(kept),
        out_specs=[VMEM_SPEC] * len(out),
        out_shape=out,
        scratch_shapes=list(scratch),
        name=name,
        cost_estimate=pl.CostEstimate(flops=flops, transcendentals=0, bytes_accessed=size),
        compiler_params=pltpu.CompilerParams(vmem_limit_bytes=8 << 20),
    )(*kept)
    return results if many else results[0]


def tails_kernel(key_hbm, query_hbm, out_ref, sems):
    width = key_hbm.shape[1]
    last = pl.ds(BLK - AUX, AUX)
    for copy in start_all(
        [
            pltpu.make_async_copy(key_hbm.at[last], out_ref.at[:, 0:width], sems.at[0]),
            pltpu.make_async_copy(query_hbm.at[last], out_ref.at[:, width : 2 * width], sems.at[1]),
        ]
    ):
        copy.wait()


def tails_call(key_raw, query_raw):
    return kernel_call(
        tails_kernel,
        [("hbm", key_raw), ("hbm", query_raw)],
        [("vmem", (AUX, 2 * key_raw.shape[1]), BF16)],
        [pltpu.SemaphoreType.DMA((2,))],
        "tails",
        0,
        1 << 17,
    )[0]


def prepare_kernel(in_hbm, forget_hbm, key_hbm, tap_hbm, val_hbm, rows_ref, key_ref, tap_ref, val_ref, gate_buf, sems):
    gates_in = start_all(
        [
            pltpu.make_async_copy(in_hbm, gate_buf.at[0], sems.at[0]),
            pltpu.make_async_copy(forget_hbm, gate_buf.at[1], sems.at[1]),
        ]
    )
    loads = start_all(
        [
            pltpu.make_async_copy(key_hbm, key_ref, sems.at[2]),
            pltpu.make_async_copy(tap_hbm, tap_ref, sems.at[3]),
            pltpu.make_async_copy(val_hbm, val_ref, sems.at[4]),
        ]
    )
    for copy in gates_in:
        copy.wait()
    gate = gate_buf[0].astype(F32)
    forget = gate_buf[1].astype(F32)
    log_forget = jnp.minimum(forget, 0.0) - jnp.log1p(jnp.exp(-jnp.abs(forget)))
    lane = lax.broadcasted_iota(jnp.int32, (HEADS, BLK), 1)
    total = log_forget
    shift = 1
    while shift < BLK:
        total = total + jnp.where(lane >= shift, pltpu.roll(total, shift, 1), 0.0)
        shift *= 2
    level = gate - total
    top = level
    shift = 1
    while shift < BLK:
        top = jnp.maximum(top, jnp.where(lane >= shift, pltpu.roll(top, shift, 1), -jnp.inf))
        shift *= 2
    last_top = top[:, BLK - 1 :]
    last_total = total[:, BLK - 1 :]
    out = (
        level,
        top,
        jnp.exp(level - last_top),
        jnp.broadcast_to(last_total + last_top, (HEADS, BLK)),
        jnp.broadcast_to(last_total, (HEADS, BLK)),
    )
    for index, part in enumerate(out):
        rows_ref[index * HEADS : (index + 1) * HEADS] = part
    for copy in loads:
        copy.wait()


def prepare_call(in_gate, forget_gate, key_raw, key_conv, values):
    return kernel_call(
        prepare_kernel,
        [("hbm", in_gate.T), ("hbm", forget_gate.T), ("hbm", key_raw), ("hbm", key_conv), ("hbm", values)],
        [
            ("vmem", (5 * HEADS, BLK), F32),
            ("vmem", key_raw.shape, BF16),
            ("vmem", key_conv.shape, BF16),
            ("vmem", values.shape, BF16),
        ],
        [pltpu.VMEM((2, HEADS, BLK), BF16), pltpu.SemaphoreType.DMA((5,))],
        "prepare",
        0,
        6 << 20,
    )


def row_of(rows_ref, kind, head):
    return rows_ref[pl.ds(kind * HEADS + head, 1), :]


PADDED = pltpu.VMEM((BLK + 8, DK), F32)
HBM_SPEC = pl.BlockSpec(memory_space=pltpu.HBM)
LIMIT = 20 << 20


def kernel_call(kernel, inputs, outputs, scratch, name, flops, size):
    in_specs, operands = [], []
    for where, x in inputs:
        operands.append(pltpu.with_memory_space_constraint(x, pltpu.VMEM if where == "vmem" else pltpu.HBM))
        in_specs.append(VMEM_SPEC if where == "vmem" else HBM_SPEC)
    return pl.pallas_call(
        kernel,
        in_specs=in_specs,
        out_specs=[VMEM_SPEC if where == "vmem" else HBM_SPEC for where, _, _ in outputs],
        out_shape=[
            (pltpu.VMEM if where == "vmem" else pltpu.HBM)(shape, dtype)
            for where, shape, dtype in outputs
        ],
        scratch_shapes=scratch,
        name=name,
        cost_estimate=pl.CostEstimate(flops=flops, transcendentals=0, bytes_accessed=size),
        compiler_params=pltpu.CompilerParams(vmem_limit_bytes=LIMIT),
    )(*operands)


def conv_rows(columns, rim_columns, raw, rim_ref, tap_ref, padded):
    padded[0:8] = rim_ref[:, rim_columns].astype(F32)[8:16]
    padded[8 : 8 + BLK] = raw.astype(F32)
    taps = tap_ref[:, columns].astype(F32)
    for start in range(0, BLK, STEP):
        first = 8 - (TAPS - 1) + start
        mixed = taps[0:1] * padded[first : first + STEP]
        for tap in range(1, TAPS):
            mixed = mixed + taps[tap : tap + 1] * padded[first + tap : first + tap + STEP]
        yield start, (mixed * (0.5 * jnp.tanh(0.5 * mixed) + 0.5)).astype(BF16)


def start_all(copies):
    for copy in copies:
        copy.start()
    return copies


def state_kernel(mine, chain, raw_ref, rim_ref, tap_ref, val_ref, rows_ref, rec_ref, padded, weighted):
    head0 = first_head(mine, chain)
    for local in range(LOCAL):
        head = head0 + local
        weight = column(row_of(rows_ref, 2, head))
        norm = jnp.zeros((1, DK), F32)
        columns = span(head, DK)
        for start, act in conv_rows(columns, columns, raw_ref[:, columns], rim_ref, tap_ref, padded.at[local % 2]):
            scaled = act.astype(F32) * widen(weight[start : start + STEP], DK)
            norm = norm + jnp.sum(scaled, axis=0, keepdims=True)
            weighted[local % 2, start : start + STEP] = scaled.astype(BF16)
        memory = lax.dot_general(
            weighted[local % 2], val_ref[:, span(head, DV)], (((0,), (0,)), ((), ())), preferred_element_type=F32
        )
        top = row_of(rows_ref, 3, head)[:, :WIDTH]
        decay = row_of(rows_ref, 4, head)[:, :WIDTH]
        aux = aux_rows([norm[:, k * WIDTH : (k + 1) * WIDTH] for k in range(SPLIT)], top, decay)
        for piece in range(PIECES):
            at = local * PIECES + piece
            rec_ref[at, 0:DK] = memory[:, piece * WIDTH : (piece + 1) * WIDTH].astype(BF16)
            rec_ref[at, DK:ROWS] = aux


def state_call(mine, chain, raw, rim, taps, values, rows):
    return kernel_call(
        functools.partial(state_kernel, mine, chain),
        [("vmem", raw), ("vmem", rim), ("vmem", taps), ("vmem", values), ("vmem", rows)],
        [("vmem", (OWNERS, ROWS, WIDTH), BF16)],
        [pltpu.VMEM((2, BLK + 8, DK), F32), pltpu.VMEM((2, BLK, DK), BF16)],
        "state",
        LOCAL * 2 * BLK * DK * DV,
        LOCAL * 3 << 20,
    )[0]


def merge(early, late):
    norms, top, decay = early
    later_norms, later_top, later_decay = late
    joined_top = jnp.maximum(top + later_decay, later_top)
    before = jnp.exp(top + later_decay - joined_top)
    after = jnp.exp(later_top - joined_top)
    joined = [before * a + after * b for a, b in zip(norms, later_norms)]
    return before, after, (joined, joined_top, decay + later_decay)


def join_kernel(own_ref, other_ref, *refs):
    outs, buf = refs[:-1], refs[-1]
    core, _, chip = place()
    second = core == 1
    for local in range(LOCAL):
        at = local * PIECES
        norms, top, decay = read_aux(own_ref[at, DK:ROWS])
        other_norms, other_top, other_decay = read_aux(other_ref[at, DK:ROWS])
        own_log = top + jnp.where(second, 0.0, other_decay)
        other_log = other_top + jnp.where(second, decay, 0.0)
        joined_top = jnp.maximum(own_log, other_log)
        own_weight = jnp.exp(own_log - joined_top)
        other_weight = jnp.exp(other_log - joined_top)
        joined = [own_weight * a + other_weight * b for a, b in zip(norms, other_norms)]
        aux = aux_rows(joined, joined_top, decay + other_decay)
        for piece in range(PIECES):
            own = own_ref[at + piece, 0:DK].astype(F32)
            other = other_ref[at + piece, 0:DK].astype(F32)
            buf[at + piece, 0:DK] = (own_weight * own + other_weight * other).astype(BF16)
            buf[at + piece, DK:ROWS] = aux
    for mask, out_ref in enumerate(outs):
        out_ref[...] = buf[chip ^ mask]


def join_call(own, other):
    return kernel_call(
        join_kernel,
        [("vmem", own), ("vmem", other)],
        [("vmem", own.shape[1:], BF16)] * OWNERS,
        [pltpu.VMEM(own.shape, BF16)],
        "join",
        0,
        4 << 20,
    )


def split_kernel(first_ref, *refs):
    records, (keep_ref, send_ref, enter_buf) = refs[:OWNERS], refs[OWNERS:]
    core, _, chip = place()
    second = core == 1
    for mask, record in enumerate(records):
        enter_buf[chip ^ mask] = record[...]
    for local in range(LOCAL):
        at = local * PIECES
        early = read_aux(enter_buf[at, DK:ROWS])
        before, after, joined = merge(early, read_aux(first_ref[at, DK:ROWS]))
        aux = aux_rows(*joined)
        plain = enter_buf[at, DK:ROWS]
        for piece in range(PIECES):
            chip_part = enter_buf[at + piece, 0:DK]
            moved = before * chip_part.astype(F32) + after * first_ref[at + piece, 0:DK].astype(F32)
            moved = moved.astype(BF16)
            keep_ref[at + piece, 0:DK] = jnp.where(second, moved, chip_part)
            send_ref[at + piece, 0:DK] = jnp.where(second, chip_part, moved)
            keep_ref[at + piece, DK:ROWS] = jnp.where(second, aux, plain)
            send_ref[at + piece, DK:ROWS] = jnp.where(second, plain, aux)


def split_call(records, first):
    shape = (OWNERS, ROWS, WIDTH)
    return kernel_call(
        split_kernel,
        [("vmem", first)] + [("vmem", record) for record in records],
        [("vmem", shape, BF16)] * 2,
        [pltpu.VMEM(shape, BF16)],
        "split",
        0,
        4 << 20,
    )


def near_kernel(
    heads, park, raw_hbm, key_hbm, rim_ref, tap_hbm, key_tap_hbm, val_hbm, rows_ref, *refs,
):
    count = len(heads)
    if park:
        own_ref, other_ref = refs[:2]
        first_hbm = refs[5]
        refs = refs[2:5] + refs[6:]
    (
        query_hbm, num_hbm, stat_ref,
        raw_buf, raw_key_buf, key_buf, val_buf, query_buf, num_buf, tap_buf, padded, sems,
    ) = refs
    places = [first_head(mine, 0) + local for mine, local in heads]
    taps_in = start_all(
        [
            pltpu.make_async_copy(tap_hbm, tap_buf.at[0], sems.at[5 * count]),
            pltpu.make_async_copy(key_tap_hbm, tap_buf.at[1], sems.at[5 * count + 1]),
        ]
    )
    if park:
        second = place()[0] == 1
        held = pltpu.make_async_copy(own_ref, first_hbm, sems.at[5 * count + 2])
        passed = pltpu.make_async_copy(other_ref, first_hbm, sems.at[5 * count + 2])

        @pl.when(second)
        def _():
            passed.start()

        @pl.when(jnp.logical_not(second))
        def _():
            held.start()

    coming, going = [], []
    for local in range(count):
        mid, wide = slice(local * DK, (local + 1) * DK), slice(local * DV, (local + 1) * DV)
        pairs = (
            (raw_hbm.at[:, span(places[local], DK)], raw_buf.at[local]),
            (key_hbm.at[:, span(places[local], DK)], raw_key_buf.at[local]),
            (val_hbm.at[:, span(places[local], DV)], val_buf.at[local]),
            (query_buf.at[local], query_hbm.at[:, mid]),
            (num_buf.at[local], num_hbm.at[:, wide]),
        )
        copies = [pltpu.make_async_copy(a, b, sems.at[5 * local + k]) for k, (a, b) in enumerate(pairs)]
        coming.append(start_all(copies[:3]))
        going.append(copies[3:])
    for copy in taps_in:
        copy.wait()
    causal = lax.broadcasted_iota(jnp.int32, (TILE, TILE), 0) >= lax.broadcasted_iota(
        jnp.int32, (TILE, TILE), 1
    )
    for local in range(count):
        head = places[local]
        coming[local][0].wait()
        columns, rim_columns = span(head, DK), span(HEADS + head, DK)
        for start, act in conv_rows(columns, rim_columns, raw_buf[local], rim_ref, tap_buf.at[0], padded.at[0]):
            query_buf[local, start : start + STEP] = act
        going[local][0].start()
        coming[local][1].wait()
        for start, act in conv_rows(columns, columns, raw_key_buf[local], rim_ref, tap_buf.at[1], padded.at[1]):
            key_buf[local, start : start + STEP] = act
        coming[local][2].wait()
        peak = row_of(rows_ref, 1, head)
        level = row_of(rows_ref, 0, head)
        peak_column = column(peak)
        scores = {
            s: lax.dot_general(query_buf[local, s:BLK], key_buf[local, s : s + TILE], NT, preferred_element_type=F32)
            for s in range(0, BLK, TILE)
        }
        for t in range(0, BLK, TILE):
            rows_peak = widen(peak_column[t : t + TILE], TILE)
            parts = []
            for s in range(0, t + TILE, TILE):
                exponent = level[:, s : s + TILE] - rows_peak
                if s == t:
                    exponent = jnp.where(causal, exponent, -jnp.inf)
                parts.append((scores[s][t - s : t - s + TILE] * (SCALE * jnp.exp(exponent))).astype(BF16))
            mixing = jnp.concatenate(parts, axis=1)
            num = jnp.dot(mixing, val_buf[local, 0 : t + TILE], preferred_element_type=F32)
            num_buf[local, t : t + TILE] = num.astype(NUM)
            added = sum(part.astype(F32) for part in parts)
            den = jnp.sum(added[:, 0:128] + added[:, 128:TILE], axis=1, keepdims=True)
            stat_ref[local, 0:1, t : t + TILE] = jnp.broadcast_to(den, (TILE, 128)).T[0:1]
        stat_ref[local, 1:2] = peak
        stat_ref[local, 2:8] = jnp.zeros((6, BLK), F32)
        going[local][1].start()
    for copies in going:
        for copy in copies:
            copy.wait()
    if park:
        held.wait()


def near_call(heads, query_raw, key_raw, rim, query_conv, key_conv, values, rows, parked=()):
    count = len(heads)
    inputs = [
        ("hbm", query_raw), ("hbm", key_raw), ("vmem", rim), ("hbm", query_conv), ("hbm", key_conv),
        ("hbm", values), ("vmem", rows),
    ]
    outputs = [
        ("hbm", (BLK, count * DK), BF16),
        ("hbm", (BLK, count * DV), NUM),
        ("vmem", (count, 8, BLK), F32),
    ]
    if parked:
        inputs += [("vmem", record) for record in parked]
        outputs += [("hbm", parked[0].shape, BF16)]
    return kernel_call(
        functools.partial(near_kernel, heads, bool(parked)),
        inputs,
        outputs,
        [
            pltpu.VMEM((count, BLK, DK), BF16),
            pltpu.VMEM((count, BLK, DK), BF16),
            pltpu.VMEM((count, BLK, DK), BF16),
            pltpu.VMEM((count, BLK, DV), BF16),
            pltpu.VMEM((count, BLK, DK), BF16),
            pltpu.VMEM((count, BLK, DV), NUM),
            pltpu.VMEM((2, TAPS, HEADS * DK), BF16),
            pltpu.VMEM((2, BLK + 8, DK), F32),
            pltpu.SemaphoreType.DMA((5 * count + 3,)),
        ],
        "near",
        count * 2 * BLK * BLK * (DK + DV),
        count * 5 << 20,
    )


def total_kernel(rule, *refs):
    records, (stack_ref, out_ref) = refs[:-2], refs[-2:]
    _, cube, chip = place()
    count = len(records)
    for mask, record in enumerate(records):
        stack_ref[mask if rule else chip ^ mask] = record[...]
    norms, tops, decays = [], [], []
    for k in range(count):
        norm, top, decay = read_aux(stack_ref[k, DK:ROWS])
        norms.append(norm)
        tops.append(jnp.where(cube > rule[k], top, EMPTY) if rule else top)
        decays.append(decay)
    after = jnp.zeros((1, WIDTH), F32)
    logs = [None] * count
    for k in reversed(range(count)):
        logs[k] = tops[k] + after
        after = after + decays[k]
    peak = functools.reduce(jnp.maximum, logs)
    weights = [jnp.exp(log - peak) for log in logs]
    joined = [sum(w * n[part] for w, n in zip(weights, norms)) for part in range(SPLIT)]
    for start in range(0, DK, STEP):
        acc = weights[0] * stack_ref[0, start : start + STEP].astype(F32)
        for k in range(1, count):
            acc = acc + weights[k] * stack_ref[k, start : start + STEP].astype(F32)
        out_ref[start : start + STEP] = acc.astype(BF16)
    out_ref[DK:ROWS] = aux_rows(joined, peak, after)


def total_call(records, rule=None):
    return kernel_call(
        functools.partial(total_kernel, rule),
        [("vmem", record) for record in records],
        [("vmem", (len(records), ROWS, WIDTH), BF16), ("vmem", (ROWS, WIDTH), BF16)],
        [],
        "total",
        0,
        1 << 20,
    )


def prefix_kernel(rec_ref, enter_ref, *refs):
    outs, buf = refs[:-1], refs[-1]
    _, cube, chip = place()
    norms, top, _ = read_aux(enter_ref[DK:ROWS])
    state = (norms, jnp.where(cube > 0, top, EMPTY), jnp.zeros((1, WIDTH), F32))
    weights = []
    for k in range(OWNERS):
        buf[k, DK:ROWS] = aux_rows(*state)
        if k + 1 < OWNERS:
            early, late, state = merge(state, read_aux(rec_ref[k, DK:ROWS]))
            weights.append((early, late))
    for start in range(0, DK, STEP):
        run = enter_ref[start : start + STEP].astype(F32)
        for k in range(OWNERS):
            buf[k, start : start + STEP] = run.astype(BF16)
            if k + 1 < OWNERS:
                early, late = weights[k]
                run = early * run + late * rec_ref[k, start : start + STEP].astype(F32)
    for mask, out_ref in enumerate(outs):
        out_ref[...] = buf[chip ^ mask]


def prefix_call(records, entering):
    return kernel_call(
        prefix_kernel,
        [("vmem", records), ("vmem", entering)],
        [("vmem", (ROWS, WIDTH), BF16)] * OWNERS,
        [pltpu.VMEM(records.shape, BF16)],
        "prefix",
        0,
        2 << 20,
    )


def far_kernel(mine, slots, sources, *refs):
    near, enter_ref, (out_ref, ready, sems) = refs[: 3 * sources], refs[3 * sources], refs[-3:]
    copies = []
    for local, (source, slot) in enumerate(slots):
        query_ref, num_ref, stat_ref = near[3 * source : 3 * source + 3]
        mid, wide = slice(slot * DK, (slot + 1) * DK), slice(slot * DV, (slot + 1) * DV)
        at = local * PIECES
        aux = enter_ref[at, DK:ROWS]
        _, far_log, _ = read_aux(aux)
        far_log = far_log[:, 0:1]
        query = query_ref[:, mid]
        den = stat_ref[slot, 0:1]
        near_peak = stat_ref[slot, 1:2]
        peak = jnp.maximum(near_peak, far_log)
        near_part = jnp.exp(near_peak - peak)
        far_part = jnp.exp(far_log - peak) * SCALE
        below = near_part * den + far_part * dot_norm(aux, query)
        scale = 1.0 / jnp.maximum(jnp.abs(below), 1.0)
        near_column = column(near_part * scale)
        far_column = column(far_part * scale)
        memory = jnp.concatenate([enter_ref[at + piece, 0:DK] for piece in range(PIECES)], axis=1)
        for t in range(0, BLK, STEP):
            far = jnp.dot(query[t : t + STEP], memory, preferred_element_type=F32)
            near_weight = widen(near_column[t : t + STEP], DV)
            far_weight = widen(far_column[t : t + STEP], DV)
            near_rows = num_ref[t : t + STEP, wide].astype(F32)
            ready[local, t : t + STEP] = (near_weight * near_rows + far_weight * far).astype(BF16)
        head = first_head(mine, 0) + local
        copies.append(pltpu.make_async_copy(ready.at[local], out_ref.at[:, span(head, DV)], sems.at[local]))
        copies[-1].start()
    for copy in copies:
        copy.wait()


def far_call(mine, near, entering, out=None):
    slots, operands = [], []
    for source, (heads, results) in enumerate(near):
        operands += results
        slots += [(local, (source, slot)) for slot, (side, local) in enumerate(heads) if side == mine]
    slots = [slot for _, slot in sorted(slots)]
    operands = [pltpu.with_memory_space_constraint(x, pltpu.VMEM) for x in operands + [entering]]
    in_specs = [VMEM_SPEC] * len(operands)
    aliases = {}
    if out is not None:
        in_specs.append(pl.BlockSpec(memory_space=pltpu.HBM))
        aliases = {len(operands): 0}
        operands.append(out)
    return pl.pallas_call(
        functools.partial(far_kernel, mine, slots, len(near)),
        in_specs=in_specs,
        out_specs=pl.BlockSpec(memory_space=pltpu.HBM),
        out_shape=jax.ShapeDtypeStruct((BLK, HEADS * DV), BF16),
        scratch_shapes=[pltpu.VMEM((LOCAL, BLK, DV), BF16), pltpu.SemaphoreType.DMA((LOCAL,))],
        input_output_aliases=aliases,
        compiler_params=pltpu.CompilerParams(vmem_limit_bytes=8 << 20),
        name="far",
        cost_estimate=pl.CostEstimate(
            flops=LOCAL * 2 * BLK * DK * DV, transcendentals=0, bytes_accessed=LOCAL * 5 << 20
        ),
    )(*operands)


def on_device(query_raw, key_raw, values, in_gate, forget_gate, query_conv, key_conv):
    devices = lax.axis_size(AXES)
    cube_size = 2 * OWNERS
    cubes = devices // cube_size
    line = [(i, i + 1) for i in range(devices - 1)]
    swap = [(i, i ^ 1) for i in range(devices)]
    up = lambda distance: [(i, i + distance * cube_size) for i in range(devices - distance * cube_size)]
    after = lambda x, *done: lax.optimization_barrier((x,) + done)[0]

    def spread(records):
        moved = {0: records[0]}
        for mask in ORDER:
            route = [(i, i ^ (2 * mask)) for i in range(devices)]
            moved[mask] = lax.ppermute(records[mask], AXES, route)
        return [moved[mask] for mask in range(OWNERS)]

    rim = lax.ppermute(tails_call(key_raw, query_raw), AXES, line)
    rows, key_held, taps_held, val_held = prepare_call(in_gate, forget_gate, key_raw, key_conv, values)
    near_args = (query_raw, key_raw, rim, query_conv, key_conv, values)

    sent = state_call(False, 0, key_held, rim, taps_held, val_held, rows)
    rows = after(rows, sent)
    other = lax.ppermute(sent, AXES, swap)
    own = state_call(True, 0, key_held, rim, taps_held, val_held, rows)
    joined = join_call(own, other)
    rows = after(rows, joined[0])
    records = spread(joined)
    *near_first, first = near_call(PARTS[0], *near_args, rows, (own, other))
    records[0] = after(records[0], near_first[0])
    stack, total = total_call(records)
    rows = after(rows, total)
    entering = lax.ppermute(total, AXES, up(1))
    distance = 1
    while distance < cubes - 1:
        earlier = lax.ppermute(entering, AXES, up(distance))
        entering = total_call([earlier, entering], (distance, 0))[1]
        distance *= 2
    near_second = near_call(PARTS[1], *near_args, rows)
    before = prefix_call(after(stack, near_second[0]), entering)
    rows = after(rows, before[0])
    records = spread(before)
    near_third = near_call(PARTS[2], *near_args, rows)
    records[0] = after(records[0], near_third[0])
    keep, send = split_call(records, first)
    enter_theirs = lax.ppermute(send, AXES, swap)
    near = list(zip(PARTS, ([*near_first], [*near_second], [*near_third])))
    sides = [[part for part in near if any(side == mine for side, _ in part[0])] for mine in (True, False)]
    out = far_call(True, sides[0], keep)
    return far_call(False, sides[1], enter_theirs, out)


def solution(mesh):
    split = P(AXES, None)
    in_specs = (split, split, split, split, split, P(), P())
    return jax.shard_map(on_device, mesh=mesh, in_specs=in_specs, out_specs=split, check_vma=False)
```

```python
import functools

import jax
import jax.numpy as jnp
from jax import lax
from jax.experimental import pallas as pl
from jax.experimental.pallas import tpu as pltpu
from jax.sharding import PartitionSpec as P

AXES = ("ctx", "head")
HEADS = 8
CHAINS = 1
GROUP = HEADS // 2
LOCAL = GROUP // CHAINS
OWNERS = 8
DK = 256
DV = 512
WIDTH = LOCAL * DV // OWNERS
PIECES = DV // WIDTH
SPLIT = DK // WIDTH
AUX = 8
RIM = 8
EARLY = 16
ROWS = DK + AUX
BLK = 512
TAPS = 4
TILE = 256
STEP = 128
EMPTY = -1e30
ORDER = (7, 6, 5, 3, 4, 2, 1)
SIDES = [(True, local) for local in range(LOCAL)] + [(False, local) for local in range(LOCAL)]
PARTS = (SIDES[:5], SIDES[5:6], SIDES[6:])
SCALE = DK**-0.5
F32 = jnp.float32
BF16 = jnp.bfloat16
NUM = BF16
NT = (((1,), (1,)), ((), ()))


def narrow(x):
    return x.astype(BF16).astype(F32)


def split3(x):
    top = narrow(x)
    middle = narrow(x - top)
    return [top, middle, x - top - middle]


def aux_rows(norms, top, decay):
    parts = []
    for norm in norms:
        high = narrow(norm)
        parts += [high, norm - high]
    parts += split3(top) + split3(decay)
    row = lax.broadcasted_iota(jnp.int32, (AUX, WIDTH), 0)
    out = jnp.zeros((AUX, WIDTH), F32)
    for index, part in enumerate(parts):
        out = jnp.where(row == index, part, out)
    return out.astype(BF16)


def read_aux(aux):
    aux = aux.astype(F32)
    norms = [aux[2 * k : 2 * k + 1] + aux[2 * k + 1 : 2 * k + 2] for k in range(SPLIT)]
    at = 2 * SPLIT
    top = aux[at : at + 1] + aux[at + 1 : at + 2] + aux[at + 2 : at + 3]
    decay = aux[at + 3 : at + 4] + aux[at + 4 : at + 5] + aux[at + 5 : at + 6]
    return norms, top, decay


def dot_norm(aux, query):
    out = None
    for k in range(SPLIT):
        part = lax.dot_general(
            aux, query[:, k * WIDTH : (k + 1) * WIDTH], NT, preferred_element_type=F32
        )
        part = part[2 * k : 2 * k + 1] + part[2 * k + 1 : 2 * k + 2]
        out = part if out is None else out + part
    return out


def column(row):
    return jnp.broadcast_to(row, (128, row.shape[1])).T


def widen(col, width):
    return jnp.concatenate([col] * (width // 128), axis=1)


def place():
    me = lax.axis_index("ctx") * lax.axis_size("head") + lax.axis_index("head")
    return me % 2, me // (2 * OWNERS), me % (2 * OWNERS) // 2


def first_head(mine, chain):
    core = place()[0]
    return GROUP * (core if mine else 1 - core) + LOCAL * chain


def span(index, width):
    return pl.ds(pl.multiple_of(index * width, width), width)


VMEM_SPEC = pl.BlockSpec(memory_space=pltpu.VMEM)


def on_chip(kernel, operands, shapes, scratch=(), name=None, flops=0, size=1 << 20):
    many = isinstance(shapes, list)
    kept = [pltpu.with_memory_space_constraint(x, pltpu.VMEM) for x in operands]
    out = [pltpu.VMEM(shape, dtype) for shape, dtype in (shapes if many else [shapes])]
    results = pl.pallas_call(
        kernel,
        in_specs=[VMEM_SPEC] * len(kept),
        out_specs=[VMEM_SPEC] * len(out),
        out_shape=out,
        scratch_shapes=list(scratch),
        name=name,
        cost_estimate=pl.CostEstimate(flops=flops, transcendentals=0, bytes_accessed=size),
        compiler_params=pltpu.CompilerParams(vmem_limit_bytes=8 << 20),
    )(*kept)
    return results if many else results[0]


def tails_kernel(key_hbm, query_hbm, out_ref, sems):
    width = key_hbm.shape[1]
    last = pl.ds(BLK - RIM, RIM)
    for copy in start_all(
        [
            pltpu.make_async_copy(key_hbm.at[last], out_ref.at[:, 0:width], sems.at[0]),
            pltpu.make_async_copy(query_hbm.at[last], out_ref.at[:, width : 2 * width], sems.at[1]),
        ]
    ):
        copy.wait()


def tails_call(key_raw, query_raw):
    return kernel_call(
        tails_kernel,
        [("hbm", key_raw), ("hbm", query_raw)],
        [("vmem", (RIM, 2 * key_raw.shape[1]), BF16)],
        [pltpu.SemaphoreType.DMA((2,))],
        "tails",
        0,
        1 << 17,
    )[0]


def prepare_kernel(in_hbm, forget_hbm, key_hbm, tap_hbm, val_hbm, rows_ref, key_ref, tap_ref, val_ref, gate_buf, sems):
    gates_in = start_all(
        [
            pltpu.make_async_copy(in_hbm, gate_buf.at[0], sems.at[0]),
            pltpu.make_async_copy(forget_hbm, gate_buf.at[1], sems.at[1]),
        ]
    )
    loads = start_all(
        [
            pltpu.make_async_copy(key_hbm, key_ref, sems.at[2]),
            pltpu.make_async_copy(tap_hbm, tap_ref, sems.at[3]),
            pltpu.make_async_copy(val_hbm, val_ref, sems.at[4]),
        ]
    )
    for copy in gates_in:
        copy.wait()
    gate = gate_buf[0].astype(F32)
    forget = gate_buf[1].astype(F32)
    log_forget = jnp.minimum(forget, 0.0) - jnp.log1p(jnp.exp(-jnp.abs(forget)))
    lane = lax.broadcasted_iota(jnp.int32, (HEADS, BLK), 1)
    total = log_forget
    shift = 1
    while shift < BLK:
        total = total + jnp.where(lane >= shift, pltpu.roll(total, shift, 1), 0.0)
        shift *= 2
    level = gate - total
    top = level
    shift = 1
    while shift < BLK:
        top = jnp.maximum(top, jnp.where(lane >= shift, pltpu.roll(top, shift, 1), -jnp.inf))
        shift *= 2
    last_top = top[:, BLK - 1 :]
    last_total = total[:, BLK - 1 :]
    out = (
        level,
        top,
        jnp.exp(level - last_top),
        jnp.broadcast_to(last_total + last_top, (HEADS, BLK)),
        jnp.broadcast_to(last_total, (HEADS, BLK)),
    )
    for index, part in enumerate(out):
        rows_ref[index * HEADS : (index + 1) * HEADS] = part
    for copy in loads:
        copy.wait()


def prepare_call(in_gate, forget_gate, key_raw, key_conv, values):
    return kernel_call(
        prepare_kernel,
        [("hbm", in_gate.T), ("hbm", forget_gate.T), ("hbm", key_raw), ("hbm", key_conv), ("hbm", values)],
        [
            ("vmem", (5 * HEADS, BLK), F32),
            ("vmem", key_raw.shape, BF16),
            ("vmem", key_conv.shape, BF16),
            ("vmem", values.shape, BF16),
        ],
        [pltpu.VMEM((2, HEADS, BLK), BF16), pltpu.SemaphoreType.DMA((5,))],
        "prepare",
        0,
        6 << 20,
    )


def row_of(rows_ref, kind, head):
    return rows_ref[pl.ds(kind * HEADS + head, 1), :]


PADDED = pltpu.VMEM((BLK + 8, DK), F32)
HBM_SPEC = pl.BlockSpec(memory_space=pltpu.HBM)
LIMIT = 20 << 20


def kernel_call(kernel, inputs, outputs, scratch, name, flops, size):
    in_specs, operands = [], []
    for where, x in inputs:
        operands.append(pltpu.with_memory_space_constraint(x, pltpu.VMEM if where == "vmem" else pltpu.HBM))
        in_specs.append(VMEM_SPEC if where == "vmem" else HBM_SPEC)
    return pl.pallas_call(
        kernel,
        in_specs=in_specs,
        out_specs=[VMEM_SPEC if where == "vmem" else HBM_SPEC for where, _, _ in outputs],
        out_shape=[
            (pltpu.VMEM if where == "vmem" else pltpu.HBM)(shape, dtype)
            for where, shape, dtype in outputs
        ],
        scratch_shapes=scratch,
        name=name,
        cost_estimate=pl.CostEstimate(flops=flops, transcendentals=0, bytes_accessed=size),
        compiler_params=pltpu.CompilerParams(vmem_limit_bytes=LIMIT),
    )(*operands)


def conv_rows(columns, rim_columns, raw, rim_ref, tap_ref, padded):
    padded[0:8] = rim_ref[:, rim_columns].astype(F32)
    padded[8 : 8 + BLK] = raw.astype(F32)
    taps = tap_ref[:, columns].astype(F32)
    for start in range(0, BLK, STEP):
        first = 8 - (TAPS - 1) + start
        mixed = taps[0:1] * padded[first : first + STEP]
        for tap in range(1, TAPS):
            mixed = mixed + taps[tap : tap + 1] * padded[first + tap : first + tap + STEP]
        yield start, (mixed * (0.5 * jnp.tanh(0.5 * mixed) + 0.5)).astype(BF16)


def start_all(copies):
    for copy in copies:
        copy.start()
    return copies


def write_record(rec_ref, local, memory, norm, top, decay):
    aux = aux_rows([norm[:, k * WIDTH : (k + 1) * WIDTH] for k in range(SPLIT)], top, decay)
    for piece in range(PIECES):
        at = local * PIECES + piece
        rec_ref[at, 0:DK] = memory[:, piece * WIDTH : (piece + 1) * WIDTH].astype(BF16)
        rec_ref[at, DK:ROWS] = aux


def outer(weighted, values):
    return lax.dot_general(weighted, values, (((0,), (0,)), ((), ())), preferred_element_type=F32)


def state_kernel(raw_ref, rim_ref, tap_ref, val_ref, rows_ref, rec_ref, act_ref, padded, weighted):
    for local in range(LOCAL):
        head = first_head(True, 0) + local
        weight = column(row_of(rows_ref, 2, head))
        norm = jnp.zeros((1, DK), F32)
        columns = span(head, DK)
        for start, act in conv_rows(columns, columns, raw_ref[:, columns], rim_ref, tap_ref, padded.at[local % 2]):
            act_ref[start : start + STEP, local * DK : (local + 1) * DK] = act
            scaled = act.astype(F32) * widen(weight[start : start + STEP], DK)
            norm = norm + jnp.sum(scaled, axis=0, keepdims=True)
            weighted[local % 2, start : start + STEP] = scaled.astype(BF16)
        memory = outer(weighted[local % 2], val_ref[:, span(head, DV)])
        top = row_of(rows_ref, 3, head)[:, :WIDTH]
        decay = row_of(rows_ref, 4, head)[:, :WIDTH]
        write_record(rec_ref, local, memory, norm, top, decay)


def state_call(raw, rim, taps, values, rows):
    return kernel_call(
        state_kernel,
        [("vmem", raw), ("vmem", rim), ("vmem", taps), ("vmem", values), ("vmem", rows)],
        [("vmem", (OWNERS, ROWS, WIDTH), BF16), ("vmem", (BLK, LOCAL * DK), BF16)],
        [pltpu.VMEM((2, BLK + 8, DK), F32), pltpu.VMEM((2, BLK, DK), BF16)],
        "state",
        LOCAL * 2 * BLK * DK * DV,
        LOCAL * 3 << 20,
    )


def late_state_kernel(raw_ref, tap_ref, val_ref, rows_ref, memory_ref, norm_ref, no_rim, padded, weighted):
    no_rim[...] = jnp.zeros((RIM, HEADS * DK), BF16)
    lanes = lax.broadcasted_iota(jnp.int32, (1, BLK), 1)
    for local in range(LOCAL):
        head = first_head(False, 0) + local
        weight = column(jnp.where(lanes >= EARLY, row_of(rows_ref, 2, head), 0.0))
        norm = jnp.zeros((1, DK), F32)
        columns = span(head, DK)
        for start, act in conv_rows(columns, columns, raw_ref[:, columns], no_rim, tap_ref, padded.at[local % 2]):
            scaled = act.astype(F32) * widen(weight[start : start + STEP], DK)
            norm = norm + jnp.sum(scaled, axis=0, keepdims=True)
            weighted[local % 2, start : start + STEP] = scaled.astype(BF16)
        memory_ref[local] = outer(weighted[local % 2], val_ref[:, span(head, DV)])
        norm_ref[local] = jnp.broadcast_to(norm, (8, DK))


def late_state_call(raw, taps, values, rows):
    return kernel_call(
        late_state_kernel,
        [("vmem", raw), ("vmem", taps), ("vmem", values), ("vmem", rows)],
        [("vmem", (LOCAL, DK, DV), F32), ("vmem", (LOCAL, 8, DK), F32)],
        [
            pltpu.VMEM((RIM, HEADS * DK), BF16),
            pltpu.VMEM((2, BLK + 8, DK), F32),
            pltpu.VMEM((2, BLK, DK), BF16),
        ],
        "late_state",
        LOCAL * 2 * BLK * DK * DV,
        LOCAL * 3 << 20,
    )


def early_state_kernel(raw_ref, rim_ref, tap_ref, val_ref, rows_ref, memory_ref, norm_ref, rec_ref, padded):
    for local in range(LOCAL):
        head = first_head(False, 0) + local
        columns = span(head, DK)
        weight = column(row_of(rows_ref, 2, head)[:, 0:128])[0:EARLY]
        padded[local, 0:8] = rim_ref[:, columns].astype(F32)
        padded[local, 8 : 8 + EARLY] = raw_ref[0:EARLY, columns].astype(F32)
        taps = tap_ref[:, columns].astype(F32)
        first = 8 - (TAPS - 1)
        mixed = taps[0:1] * padded[local, first : first + EARLY]
        for tap in range(1, TAPS):
            mixed = mixed + taps[tap : tap + 1] * padded[local, first + tap : first + tap + EARLY]
        act = (mixed * (0.5 * jnp.tanh(0.5 * mixed) + 0.5)).astype(BF16)
        scaled = act.astype(F32) * widen(weight, DK)
        norm = norm_ref[local, 0:1] + jnp.sum(scaled, axis=0, keepdims=True)
        memory = memory_ref[local] + outer(scaled.astype(BF16), val_ref[0:EARLY, span(head, DV)])
        top = row_of(rows_ref, 3, head)[:, :WIDTH]
        decay = row_of(rows_ref, 4, head)[:, :WIDTH]
        write_record(rec_ref, local, memory, norm, top, decay)


def early_state_call(raw, rim, taps, values, rows, memory, norm):
    return kernel_call(
        early_state_kernel,
        [("vmem", x) for x in (raw, rim, taps, values, rows, memory, norm)],
        [("vmem", (OWNERS, ROWS, WIDTH), BF16)],
        [pltpu.VMEM((LOCAL, 8 + EARLY, DK), F32)],
        "early_state",
        1 << 20,
        4 << 20,
    )[0]


def merge(early, late):
    norms, top, decay = early
    later_norms, later_top, later_decay = late
    joined_top = jnp.maximum(top + later_decay, later_top)
    before = jnp.exp(top + later_decay - joined_top)
    after = jnp.exp(later_top - joined_top)
    joined = [before * a + after * b for a, b in zip(norms, later_norms)]
    return before, after, (joined, joined_top, decay + later_decay)


def join_kernel(own_ref, other_ref, *refs):
    outs, buf = refs[:-1], refs[-1]
    core, _, chip = place()
    second = core == 1
    for local in range(LOCAL):
        at = local * PIECES
        norms, top, decay = read_aux(own_ref[at, DK:ROWS])
        other_norms, other_top, other_decay = read_aux(other_ref[at, DK:ROWS])
        own_log = top + jnp.where(second, 0.0, other_decay)
        other_log = other_top + jnp.where(second, decay, 0.0)
        joined_top = jnp.maximum(own_log, other_log)
        own_weight = jnp.exp(own_log - joined_top)
        other_weight = jnp.exp(other_log - joined_top)
        joined = [own_weight * a + other_weight * b for a, b in zip(norms, other_norms)]
        aux = aux_rows(joined, joined_top, decay + other_decay)
        for piece in range(PIECES):
            own = own_ref[at + piece, 0:DK].astype(F32)
            other = other_ref[at + piece, 0:DK].astype(F32)
            buf[at + piece, 0:DK] = (own_weight * own + other_weight * other).astype(BF16)
            buf[at + piece, DK:ROWS] = aux
    for mask, out_ref in enumerate(outs):
        out_ref[...] = buf[chip ^ mask]


def join_call(own, other):
    return kernel_call(
        join_kernel,
        [("vmem", own), ("vmem", other)],
        [("vmem", own.shape[1:], BF16)] * OWNERS,
        [pltpu.VMEM(own.shape, BF16)],
        "join",
        0,
        4 << 20,
    )


def split_kernel(first_ref, *refs):
    records, (keep_ref, send_ref, enter_buf) = refs[:OWNERS], refs[OWNERS:]
    core, _, chip = place()
    second = core == 1
    for mask, record in enumerate(records):
        enter_buf[chip ^ mask] = record[...]
    for local in range(LOCAL):
        at = local * PIECES
        early = read_aux(enter_buf[at, DK:ROWS])
        before, after, joined = merge(early, read_aux(first_ref[at, DK:ROWS]))
        aux = aux_rows(*joined)
        plain = enter_buf[at, DK:ROWS]
        for piece in range(PIECES):
            chip_part = enter_buf[at + piece, 0:DK]
            moved = before * chip_part.astype(F32) + after * first_ref[at + piece, 0:DK].astype(F32)
            moved = moved.astype(BF16)
            keep_ref[at + piece, 0:DK] = jnp.where(second, moved, chip_part)
            send_ref[at + piece, 0:DK] = jnp.where(second, chip_part, moved)
            keep_ref[at + piece, DK:ROWS] = jnp.where(second, aux, plain)
            send_ref[at + piece, DK:ROWS] = jnp.where(second, plain, aux)


def split_call(records, first):
    shape = (OWNERS, ROWS, WIDTH)
    return kernel_call(
        split_kernel,
        [("vmem", first)] + [("vmem", record) for record in records],
        [("vmem", shape, BF16)] * 2,
        [pltpu.VMEM(shape, BF16)],
        "split",
        0,
        4 << 20,
    )


def near_kernel(
    heads, park, raw_hbm, key_hbm, rim_ref, tap_hbm, key_tap_hbm, val_hbm, rows_ref, *refs,
):
    count = len(heads)
    if park:
        own_ref, other_ref, act_ref = refs[:3]
        first_hbm = refs[6]
        refs = refs[3:6] + refs[7:]
    (
        query_hbm, num_hbm, stat_ref,
        raw_buf, raw_key_buf, key_buf, val_buf, query_buf, num_buf, tap_buf, padded, sems,
    ) = refs
    places = [first_head(mine, 0) + local for mine, local in heads]
    taps_in = start_all(
        [
            pltpu.make_async_copy(tap_hbm, tap_buf.at[0], sems.at[5 * count]),
            pltpu.make_async_copy(key_tap_hbm, tap_buf.at[1], sems.at[5 * count + 1]),
        ]
    )
    if park:
        second = place()[0] == 1
        held = pltpu.make_async_copy(own_ref, first_hbm, sems.at[5 * count + 2])
        passed = pltpu.make_async_copy(other_ref, first_hbm, sems.at[5 * count + 2])

        @pl.when(second)
        def _():
            passed.start()

        @pl.when(jnp.logical_not(second))
        def _():
            held.start()

    coming, going = [], []
    for local in range(count):
        mid, wide = slice(local * DK, (local + 1) * DK), slice(local * DV, (local + 1) * DV)
        pairs = (
            (raw_hbm.at[:, span(places[local], DK)], raw_buf.at[local]),
            (key_hbm.at[:, span(places[local], DK)], raw_key_buf.at[local]),
            (val_hbm.at[:, span(places[local], DV)], val_buf.at[local]),
            (query_buf.at[local], query_hbm.at[:, mid]),
            (num_buf.at[local], num_hbm.at[:, wide]),
        )
        copies = [pltpu.make_async_copy(a, b, sems.at[5 * local + k]) for k, (a, b) in enumerate(pairs)]
        held_key = park and heads[local][0]
        coming.append(start_all(copies[:1] + copies[2:3] if held_key else copies[:3]))
        going.append(copies[3:])
    for copy in taps_in:
        copy.wait()
    causal = lax.broadcasted_iota(jnp.int32, (TILE, TILE), 0) >= lax.broadcasted_iota(
        jnp.int32, (TILE, TILE), 1
    )
    for local in range(count):
        head = places[local]
        coming[local][0].wait()
        columns, rim_columns = span(head, DK), span(HEADS + head, DK)
        for start, act in conv_rows(columns, rim_columns, raw_buf[local], rim_ref, tap_buf.at[0], padded.at[0]):
            query_buf[local, start : start + STEP] = act
        going[local][0].start()
        if park and heads[local][0]:
            key_act = act_ref.at[:, (local * DK) : (local + 1) * DK]
        else:
            coming[local][1].wait()
            for start, act in conv_rows(columns, columns, raw_key_buf[local], rim_ref, tap_buf.at[1], padded.at[1]):
                key_buf[local, start : start + STEP] = act
            key_act = key_buf.at[local]
        coming[local][-1].wait()
        peak = row_of(rows_ref, 1, head)
        level = row_of(rows_ref, 0, head)
        peak_column = column(peak)
        scores = {
            s: lax.dot_general(query_buf[local, s:BLK], key_act[s : s + TILE], NT, preferred_element_type=F32)
            for s in range(0, BLK, TILE)
        }
        for t in range(0, BLK, TILE):
            rows_peak = widen(peak_column[t : t + TILE], TILE)
            parts = []
            for s in range(0, t + TILE, TILE):
                exponent = level[:, s : s + TILE] - rows_peak
                if s == t:
                    exponent = jnp.where(causal, exponent, -jnp.inf)
                parts.append((scores[s][t - s : t - s + TILE] * (SCALE * jnp.exp(exponent))).astype(BF16))
            mixing = jnp.concatenate(parts, axis=1)
            num = jnp.dot(mixing, val_buf[local, 0 : t + TILE], preferred_element_type=F32)
            num_buf[local, t : t + TILE] = num.astype(NUM)
            added = sum(part.astype(F32) for part in parts)
            den = jnp.sum(added[:, 0:128] + added[:, 128:TILE], axis=1, keepdims=True)
            stat_ref[local, 0:1, t : t + TILE] = jnp.broadcast_to(den, (TILE, 128)).T[0:1]
        stat_ref[local, 1:2] = peak
        stat_ref[local, 2:8] = jnp.zeros((6, BLK), F32)
        going[local][1].start()
    for copies in going:
        for copy in copies:
            copy.wait()
    if park:
        held.wait()


def near_call(heads, query_raw, key_raw, rim, query_conv, key_conv, values, rows, parked=()):
    count = len(heads)
    inputs = [
        ("hbm", query_raw), ("hbm", key_raw), ("vmem", rim), ("hbm", query_conv), ("hbm", key_conv),
        ("hbm", values), ("vmem", rows),
    ]
    outputs = [
        ("hbm", (BLK, count * DK), BF16),
        ("hbm", (BLK, count * DV), NUM),
        ("vmem", (count, 8, BLK), F32),
    ]
    if parked:
        inputs += [("vmem", record) for record in parked]
        outputs += [("hbm", parked[0].shape, BF16)]
    return kernel_call(
        functools.partial(near_kernel, heads, bool(parked)),
        inputs,
        outputs,
        [
            pltpu.VMEM((count, BLK, DK), BF16),
            pltpu.VMEM((count, BLK, DK), BF16),
            pltpu.VMEM((count, BLK, DK), BF16),
            pltpu.VMEM((count, BLK, DV), BF16),
            pltpu.VMEM((count, BLK, DK), BF16),
            pltpu.VMEM((count, BLK, DV), NUM),
            pltpu.VMEM((2, TAPS, HEADS * DK), BF16),
            pltpu.VMEM((2, BLK + 8, DK), F32),
            pltpu.SemaphoreType.DMA((5 * count + 3,)),
        ],
        "near",
        count * 2 * BLK * BLK * (DK + DV),
        count * 5 << 20,
    )


def total_kernel(rule, *refs):
    records, (stack_ref, out_ref) = refs[:-2], refs[-2:]
    _, cube, chip = place()
    count = len(records)
    for mask, record in enumerate(records):
        stack_ref[mask if rule else chip ^ mask] = record[...]
    norms, tops, decays = [], [], []
    for k in range(count):
        norm, top, decay = read_aux(stack_ref[k, DK:ROWS])
        norms.append(norm)
        tops.append(jnp.where(cube > rule[k], top, EMPTY) if rule else top)
        decays.append(decay)
    after = jnp.zeros((1, WIDTH), F32)
    logs = [None] * count
    for k in reversed(range(count)):
        logs[k] = tops[k] + after
        after = after + decays[k]
    peak = functools.reduce(jnp.maximum, logs)
    weights = [jnp.exp(log - peak) for log in logs]
    joined = [sum(w * n[part] for w, n in zip(weights, norms)) for part in range(SPLIT)]
    for start in range(0, DK, STEP):
        acc = weights[0] * stack_ref[0, start : start + STEP].astype(F32)
        for k in range(1, count):
            acc = acc + weights[k] * stack_ref[k, start : start + STEP].astype(F32)
        out_ref[start : start + STEP] = acc.astype(BF16)
    out_ref[DK:ROWS] = aux_rows(joined, peak, after)


def total_call(records, rule=None):
    return kernel_call(
        functools.partial(total_kernel, rule),
        [("vmem", record) for record in records],
        [("vmem", (len(records), ROWS, WIDTH), BF16), ("vmem", (ROWS, WIDTH), BF16)],
        [],
        "total",
        0,
        1 << 20,
    )


def prefix_kernel(rec_ref, enter_ref, *refs):
    outs, buf = refs[:-1], refs[-1]
    _, cube, chip = place()
    norms, top, _ = read_aux(enter_ref[DK:ROWS])
    state = (norms, jnp.where(cube > 0, top, EMPTY), jnp.zeros((1, WIDTH), F32))
    weights = []
    for k in range(OWNERS):
        buf[k, DK:ROWS] = aux_rows(*state)
        if k + 1 < OWNERS:
            early, late, state = merge(state, read_aux(rec_ref[k, DK:ROWS]))
            weights.append((early, late))
    for start in range(0, DK, STEP):
        run = enter_ref[start : start + STEP].astype(F32)
        for k in range(OWNERS):
            buf[k, start : start + STEP] = run.astype(BF16)
            if k + 1 < OWNERS:
                early, late = weights[k]
                run = early * run + late * rec_ref[k, start : start + STEP].astype(F32)
    for mask, out_ref in enumerate(outs):
        out_ref[...] = buf[chip ^ mask]


def prefix_call(records, entering):
    return kernel_call(
        prefix_kernel,
        [("vmem", records), ("vmem", entering)],
        [("vmem", (ROWS, WIDTH), BF16)] * OWNERS,
        [pltpu.VMEM(records.shape, BF16)],
        "prefix",
        0,
        2 << 20,
    )


def far_kernel(mine, slots, sources, *refs):
    near, enter_ref, (out_ref, ready, sems) = refs[: 3 * sources], refs[3 * sources], refs[-3:]
    copies = []
    for local, (source, slot) in enumerate(slots):
        query_ref, num_ref, stat_ref = near[3 * source : 3 * source + 3]
        mid, wide = slice(slot * DK, (slot + 1) * DK), slice(slot * DV, (slot + 1) * DV)
        at = local * PIECES
        aux = enter_ref[at, DK:ROWS]
        _, far_log, _ = read_aux(aux)
        far_log = far_log[:, 0:1]
        query = query_ref[:, mid]
        den = stat_ref[slot, 0:1]
        near_peak = stat_ref[slot, 1:2]
        peak = jnp.maximum(near_peak, far_log)
        near_part = jnp.exp(near_peak - peak)
        far_part = jnp.exp(far_log - peak) * SCALE
        below = near_part * den + far_part * dot_norm(aux, query)
        scale = 1.0 / jnp.maximum(jnp.abs(below), 1.0)
        near_column = column(near_part * scale)
        far_column = column(far_part * scale)
        memory = jnp.concatenate([enter_ref[at + piece, 0:DK] for piece in range(PIECES)], axis=1)
        for t in range(0, BLK, STEP):
            far = jnp.dot(query[t : t + STEP], memory, preferred_element_type=F32)
            near_weight = widen(near_column[t : t + STEP], DV)
            far_weight = widen(far_column[t : t + STEP], DV)
            near_rows = num_ref[t : t + STEP, wide].astype(F32)
            ready[local, t : t + STEP] = (near_weight * near_rows + far_weight * far).astype(BF16)
        head = first_head(mine, 0) + local
        copies.append(pltpu.make_async_copy(ready.at[local], out_ref.at[:, span(head, DV)], sems.at[local]))
        copies[-1].start()
    for copy in copies:
        copy.wait()


def far_call(mine, near, entering, out=None):
    slots, operands = [], []
    for source, (heads, results) in enumerate(near):
        operands += results
        slots += [(local, (source, slot)) for slot, (side, local) in enumerate(heads) if side == mine]
    slots = [slot for _, slot in sorted(slots)]
    operands = [pltpu.with_memory_space_constraint(x, pltpu.VMEM) for x in operands + [entering]]
    in_specs = [VMEM_SPEC] * len(operands)
    aliases = {}
    if out is not None:
        in_specs.append(pl.BlockSpec(memory_space=pltpu.HBM))
        aliases = {len(operands): 0}
        operands.append(out)
    return pl.pallas_call(
        functools.partial(far_kernel, mine, slots, len(near)),
        in_specs=in_specs,
        out_specs=pl.BlockSpec(memory_space=pltpu.HBM),
        out_shape=jax.ShapeDtypeStruct((BLK, HEADS * DV), BF16),
        scratch_shapes=[pltpu.VMEM((LOCAL, BLK, DV), BF16), pltpu.SemaphoreType.DMA((LOCAL,))],
        input_output_aliases=aliases,
        compiler_params=pltpu.CompilerParams(vmem_limit_bytes=8 << 20),
        name="far",
        cost_estimate=pl.CostEstimate(
            flops=LOCAL * 2 * BLK * DK * DV, transcendentals=0, bytes_accessed=LOCAL * 5 << 20
        ),
    )(*operands)


def on_device(query_raw, key_raw, values, in_gate, forget_gate, query_conv, key_conv):
    devices = lax.axis_size(AXES)
    cube_size = 2 * OWNERS
    cubes = devices // cube_size
    line = [(i, i + 1) for i in range(devices - 1)]
    swap = [(i, i ^ 1) for i in range(devices)]
    up = lambda distance: [(i, i + distance * cube_size) for i in range(devices - distance * cube_size)]
    after = lambda x, *done: lax.optimization_barrier((x,) + done)[0]

    def spread(records):
        moved = {0: records[0]}
        for mask in ORDER:
            route = [(i, i ^ (2 * mask)) for i in range(devices)]
            moved[mask] = lax.ppermute(records[mask], AXES, route)
        return [moved[mask] for mask in range(OWNERS)]

    rim = lax.ppermute(tails_call(key_raw, query_raw), AXES, line)
    rows, key_held, taps_held, val_held = prepare_call(in_gate, forget_gate, key_raw, key_conv, values)
    near_args = (query_raw, key_raw, rim, query_conv, key_conv, values)

    late = late_state_call(key_held, taps_held, val_held, rows)
    sent = early_state_call(key_held, rim, taps_held, val_held, rows, *late)
    rows = after(rows, sent)
    other = lax.ppermute(sent, AXES, swap)
    own, key_act = state_call(key_held, rim, taps_held, val_held, rows)
    joined = join_call(own, other)
    rows = after(rows, joined[0])
    records = spread(joined)
    *near_first, first = near_call(PARTS[0], *near_args, rows, (own, other, key_act))
    records[0] = after(records[0], near_first[0])
    stack, total = total_call(records)
    rows = after(rows, total)
    entering = lax.ppermute(total, AXES, up(1))
    distance = 1
    while distance < cubes - 1:
        earlier = lax.ppermute(entering, AXES, up(distance))
        entering = total_call([earlier, entering], (distance, 0))[1]
        distance *= 2
    near_second = near_call(PARTS[1], *near_args, rows)
    before = prefix_call(after(stack, near_second[0]), entering)
    rows = after(rows, before[0])
    records = spread(before)
    near_third = near_call(PARTS[2], *near_args, rows)
    records[0] = after(records[0], near_third[0])
    keep, send = split_call(records, first)
    enter_theirs = lax.ppermute(send, AXES, swap)
    near = list(zip(PARTS, ([*near_first], [*near_second], [*near_third])))
    sides = [[part for part in near if any(side == mine for side, _ in part[0])] for mine in (True, False)]
    out = far_call(True, sides[0], keep)
    return far_call(False, sides[1], enter_theirs, out)


def solution(mesh):
    split = P(AXES, None)
    in_specs = (split, split, split, split, split, P(), P())
    return jax.shard_map(on_device, mesh=mesh, in_specs=in_specs, out_specs=split, check_vma=False)
```

```python
import functools

import jax
import jax.numpy as jnp
from jax import lax
from jax.experimental import pallas as pl
from jax.experimental.pallas import tpu as pltpu
from jax.sharding import PartitionSpec as P

AXES = ("ctx", "head")
HEADS = 8
CHAINS = 1
GROUP = HEADS // 2
LOCAL = GROUP // CHAINS
OWNERS = 8
DK = 256
DV = 512
WIDTH = LOCAL * DV // OWNERS
PIECES = DV // WIDTH
SPLIT = DK // WIDTH
AUX = 8
RIM = 8
EARLY = 16
ROWS = DK + AUX
BLK = 512
TAPS = 4
TILE = 256
STEP = 128
EMPTY = -1e30
ORDER = (7, 6, 5, 3, 4, 2, 1)
SIDES = [(True, local) for local in range(LOCAL)] + [(False, local) for local in range(LOCAL)]
PARTS = (SIDES[:5], SIDES[5:6], SIDES[6:])
SCALE = DK**-0.5
F32 = jnp.float32
BF16 = jnp.bfloat16
NUM = BF16
NT = (((1,), (1,)), ((), ()))


def narrow(x):
    return x.astype(BF16).astype(F32)


def split3(x):
    top = narrow(x)
    middle = narrow(x - top)
    return [top, middle, x - top - middle]


def aux_rows(norms, top, decay):
    parts = []
    for norm in norms:
        high = narrow(norm)
        parts += [high, norm - high]
    parts += split3(top) + split3(decay)
    row = lax.broadcasted_iota(jnp.int32, (AUX, WIDTH), 0)
    out = jnp.zeros((AUX, WIDTH), F32)
    for index, part in enumerate(parts):
        out = jnp.where(row == index, part, out)
    return out.astype(BF16)


def read_aux(aux):
    aux = aux.astype(F32)
    norms = [aux[2 * k : 2 * k + 1] + aux[2 * k + 1 : 2 * k + 2] for k in range(SPLIT)]
    at = 2 * SPLIT
    top = aux[at : at + 1] + aux[at + 1 : at + 2] + aux[at + 2 : at + 3]
    decay = aux[at + 3 : at + 4] + aux[at + 4 : at + 5] + aux[at + 5 : at + 6]
    return norms, top, decay


def dot_norm(aux, query):
    out = None
    for k in range(SPLIT):
        part = lax.dot_general(
            aux, query[:, k * WIDTH : (k + 1) * WIDTH], NT, preferred_element_type=F32
        )
        part = part[2 * k : 2 * k + 1] + part[2 * k + 1 : 2 * k + 2]
        out = part if out is None else out + part
    return out


def column(row):
    return jnp.broadcast_to(row, (128, row.shape[1])).T


def widen(col, width):
    return jnp.concatenate([col] * (width // 128), axis=1)


def place():
    me = lax.axis_index("ctx") * lax.axis_size("head") + lax.axis_index("head")
    return me % 2, me // (2 * OWNERS), me % (2 * OWNERS) // 2


def first_head(mine, chain):
    core = place()[0]
    return GROUP * (core if mine else 1 - core) + LOCAL * chain


def span(index, width):
    return pl.ds(pl.multiple_of(index * width, width), width)


VMEM_SPEC = pl.BlockSpec(memory_space=pltpu.VMEM)


def tails_kernel(key_hbm, query_hbm, out_ref, sems):
    width = key_hbm.shape[1]
    last = pl.ds(BLK - RIM, RIM)
    for copy in start_all(
        [
            pltpu.make_async_copy(key_hbm.at[last], out_ref.at[:, 0:width], sems.at[0]),
            pltpu.make_async_copy(query_hbm.at[last], out_ref.at[:, width : 2 * width], sems.at[1]),
        ]
    ):
        copy.wait()


def tails_call(key_raw, query_raw):
    return kernel_call(
        tails_kernel,
        [("hbm", key_raw), ("hbm", query_raw)],
        [("vmem", (RIM, 2 * key_raw.shape[1]), BF16)],
        [pltpu.SemaphoreType.DMA((2,))],
        "tails",
        0,
        1 << 17,
    )[0]


def prepare_kernel(in_hbm, forget_hbm, key_hbm, tap_hbm, val_hbm, rows_ref, key_ref, tap_ref, val_ref, gate_buf, sems):
    gates_in = start_all(
        [
            pltpu.make_async_copy(in_hbm, gate_buf.at[0], sems.at[0]),
            pltpu.make_async_copy(forget_hbm, gate_buf.at[1], sems.at[1]),
        ]
    )
    loads = start_all(
        [
            pltpu.make_async_copy(key_hbm, key_ref, sems.at[2]),
            pltpu.make_async_copy(tap_hbm, tap_ref, sems.at[3]),
            pltpu.make_async_copy(val_hbm, val_ref, sems.at[4]),
        ]
    )
    for copy in gates_in:
        copy.wait()
    gate = gate_buf[0].astype(F32)
    forget = gate_buf[1].astype(F32)
    log_forget = jnp.minimum(forget, 0.0) - jnp.log1p(jnp.exp(-jnp.abs(forget)))
    lane = lax.broadcasted_iota(jnp.int32, (HEADS, BLK), 1)
    total = log_forget
    shift = 1
    while shift < BLK:
        total = total + jnp.where(lane >= shift, pltpu.roll(total, shift, 1), 0.0)
        shift *= 2
    level = gate - total
    top = level
    shift = 1
    while shift < BLK:
        top = jnp.maximum(top, jnp.where(lane >= shift, pltpu.roll(top, shift, 1), -jnp.inf))
        shift *= 2
    last_top = top[:, BLK - 1 :]
    last_total = total[:, BLK - 1 :]
    out = (
        level,
        top,
        jnp.exp(level - last_top),
        jnp.broadcast_to(last_total + last_top, (HEADS, BLK)),
        jnp.broadcast_to(last_total, (HEADS, BLK)),
    )
    for index, part in enumerate(out):
        rows_ref[index * HEADS : (index + 1) * HEADS] = part
    for copy in loads:
        copy.wait()


def prepare_call(in_gate, forget_gate, key_raw, key_conv, values):
    return kernel_call(
        prepare_kernel,
        [("hbm", in_gate.T), ("hbm", forget_gate.T), ("hbm", key_raw), ("hbm", key_conv), ("hbm", values)],
        [
            ("vmem", (5 * HEADS, BLK), F32),
            ("vmem", key_raw.shape, BF16),
            ("vmem", key_conv.shape, BF16),
            ("vmem", values.shape, BF16),
        ],
        [pltpu.VMEM((2, HEADS, BLK), BF16), pltpu.SemaphoreType.DMA((5,))],
        "prepare",
        0,
        6 << 20,
    )


def row_of(rows_ref, kind, head):
    return rows_ref[pl.ds(kind * HEADS + head, 1), :]


HBM_SPEC = pl.BlockSpec(memory_space=pltpu.HBM)
LIMIT = 20 << 20


def kernel_call(kernel, inputs, outputs, scratch, name, flops, size):
    in_specs, operands = [], []
    for where, x in inputs:
        operands.append(pltpu.with_memory_space_constraint(x, pltpu.VMEM if where == "vmem" else pltpu.HBM))
        in_specs.append(VMEM_SPEC if where == "vmem" else HBM_SPEC)
    return pl.pallas_call(
        kernel,
        in_specs=in_specs,
        out_specs=[VMEM_SPEC if where == "vmem" else HBM_SPEC for where, _, _ in outputs],
        out_shape=[
            (pltpu.VMEM if where == "vmem" else pltpu.HBM)(shape, dtype)
            for where, shape, dtype in outputs
        ],
        scratch_shapes=scratch,
        name=name,
        cost_estimate=pl.CostEstimate(flops=flops, transcendentals=0, bytes_accessed=size),
        compiler_params=pltpu.CompilerParams(vmem_limit_bytes=LIMIT),
    )(*operands)


def conv_rows(columns, rim_columns, raw, rim_ref, tap_ref):
    taps = 0.5 * tap_ref[:, columns].astype(F32)
    earlier = rim_ref[:, rim_columns].astype(F32)
    for start in range(0, BLK, STEP):
        here = raw[start : start + STEP].astype(F32)
        wide = jnp.concatenate([earlier, here], axis=0)
        first = 8 - (TAPS - 1)
        mixed = taps[0:1] * wide[first : first + STEP]
        for tap in range(1, TAPS):
            mixed = mixed + taps[tap : tap + 1] * wide[first + tap : first + tap + STEP]
        earlier = here[STEP - 8 :]
        yield start, (mixed * (jnp.tanh(mixed) + 1.0)).astype(BF16)


def start_all(copies):
    for copy in copies:
        copy.start()
    return copies


def write_record(rec_ref, local, memory, norm, top, decay):
    aux = aux_rows([norm[:, k * WIDTH : (k + 1) * WIDTH] for k in range(SPLIT)], top, decay)
    for piece in range(PIECES):
        at = local * PIECES + piece
        rec_ref[at, 0:DK] = memory[:, piece * WIDTH : (piece + 1) * WIDTH].astype(BF16)
        rec_ref[at, DK:ROWS] = aux


def outer(weighted, values):
    return lax.dot_general(weighted, values, (((0,), (0,)), ((), ())), preferred_element_type=F32)


def state_kernel(raw_ref, rim_ref, tap_ref, val_ref, rows_ref, rec_ref, act_ref, weighted):
    for local in range(LOCAL):
        head = first_head(True, 0) + local
        weight = column(row_of(rows_ref, 2, head))
        norm = jnp.zeros((1, DK), F32)
        columns = span(head, DK)
        for start, act in conv_rows(columns, columns, raw_ref[:, columns], rim_ref, tap_ref):
            act_ref[start : start + STEP, local * DK : (local + 1) * DK] = act
            scaled = act.astype(F32) * widen(weight[start : start + STEP], DK)
            norm = norm + jnp.sum(scaled, axis=0, keepdims=True)
            weighted[local % 2, start : start + STEP] = scaled.astype(BF16)
        memory = outer(weighted[local % 2], val_ref[:, span(head, DV)])
        top = row_of(rows_ref, 3, head)[:, :WIDTH]
        decay = row_of(rows_ref, 4, head)[:, :WIDTH]
        write_record(rec_ref, local, memory, norm, top, decay)


def state_call(raw, rim, taps, values, rows):
    return kernel_call(
        state_kernel,
        [("vmem", raw), ("vmem", rim), ("vmem", taps), ("vmem", values), ("vmem", rows)],
        [("vmem", (OWNERS, ROWS, WIDTH), BF16), ("vmem", (BLK, LOCAL * DK), BF16)],
        [pltpu.VMEM((2, BLK, DK), BF16)],
        "state",
        LOCAL * 2 * BLK * DK * DV,
        LOCAL * 3 << 20,
    )


def late_state_kernel(raw_ref, tap_ref, val_ref, rows_ref, memory_ref, norm_ref, no_rim, weighted):
    no_rim[...] = jnp.zeros((RIM, HEADS * DK), BF16)
    lanes = lax.broadcasted_iota(jnp.int32, (1, BLK), 1)
    for local in range(LOCAL):
        head = first_head(False, 0) + local
        weight = column(jnp.where(lanes >= EARLY, row_of(rows_ref, 2, head), 0.0))
        norm = jnp.zeros((1, DK), F32)
        columns = span(head, DK)
        for start, act in conv_rows(columns, columns, raw_ref[:, columns], no_rim, tap_ref):
            scaled = act.astype(F32) * widen(weight[start : start + STEP], DK)
            norm = norm + jnp.sum(scaled, axis=0, keepdims=True)
            weighted[local % 2, start : start + STEP] = scaled.astype(BF16)
        memory_ref[local] = outer(weighted[local % 2], val_ref[:, span(head, DV)])
        norm_ref[local] = jnp.broadcast_to(norm, (8, DK))


def late_state_call(raw, taps, values, rows):
    return kernel_call(
        late_state_kernel,
        [("vmem", raw), ("vmem", taps), ("vmem", values), ("vmem", rows)],
        [("vmem", (LOCAL, DK, DV), F32), ("vmem", (LOCAL, 8, DK), F32)],
        [
            pltpu.VMEM((RIM, HEADS * DK), BF16),
            pltpu.VMEM((2, BLK, DK), BF16),
        ],
        "late_state",
        LOCAL * 2 * BLK * DK * DV,
        LOCAL * 3 << 20,
    )


def early_state_kernel(raw_ref, rim_ref, tap_ref, val_ref, rows_ref, memory_ref, norm_ref, rec_ref, padded):
    for local in range(LOCAL):
        head = first_head(False, 0) + local
        columns = span(head, DK)
        weight = column(row_of(rows_ref, 2, head)[:, 0:128])[0:EARLY]
        padded[local, 0:8] = rim_ref[:, columns].astype(F32)
        padded[local, 8 : 8 + EARLY] = raw_ref[0:EARLY, columns].astype(F32)
        taps = 0.5 * tap_ref[:, columns].astype(F32)
        first = 8 - (TAPS - 1)
        mixed = taps[0:1] * padded[local, first : first + EARLY]
        for tap in range(1, TAPS):
            mixed = mixed + taps[tap : tap + 1] * padded[local, first + tap : first + tap + EARLY]
        act = (mixed * (jnp.tanh(mixed) + 1.0)).astype(BF16)
        scaled = act.astype(F32) * widen(weight, DK)
        norm = norm_ref[local, 0:1] + jnp.sum(scaled, axis=0, keepdims=True)
        memory = memory_ref[local] + outer(scaled.astype(BF16), val_ref[0:EARLY, span(head, DV)])
        top = row_of(rows_ref, 3, head)[:, :WIDTH]
        decay = row_of(rows_ref, 4, head)[:, :WIDTH]
        write_record(rec_ref, local, memory, norm, top, decay)


def early_state_call(raw, rim, taps, values, rows, memory, norm):
    return kernel_call(
        early_state_kernel,
        [("vmem", x) for x in (raw, rim, taps, values, rows, memory, norm)],
        [("vmem", (OWNERS, ROWS, WIDTH), BF16)],
        [pltpu.VMEM((LOCAL, 8 + EARLY, DK), F32)],
        "early_state",
        1 << 20,
        4 << 20,
    )[0]


def merge(early, late):
    norms, top, decay = early
    later_norms, later_top, later_decay = late
    joined_top = jnp.maximum(top + later_decay, later_top)
    before = jnp.exp(top + later_decay - joined_top)
    after = jnp.exp(later_top - joined_top)
    joined = [before * a + after * b for a, b in zip(norms, later_norms)]
    return before, after, (joined, joined_top, decay + later_decay)


def join_kernel(own_ref, other_ref, *refs):
    outs, buf = refs[:-1], refs[-1]
    core, _, chip = place()
    second = core == 1
    for local in range(LOCAL):
        at = local * PIECES
        norms, top, decay = read_aux(own_ref[at, DK:ROWS])
        other_norms, other_top, other_decay = read_aux(other_ref[at, DK:ROWS])
        own_log = top + jnp.where(second, 0.0, other_decay)
        other_log = other_top + jnp.where(second, decay, 0.0)
        joined_top = jnp.maximum(own_log, other_log)
        own_weight = jnp.exp(own_log - joined_top)
        other_weight = jnp.exp(other_log - joined_top)
        joined = [own_weight * a + other_weight * b for a, b in zip(norms, other_norms)]
        aux = aux_rows(joined, joined_top, decay + other_decay)
        for piece in range(PIECES):
            own = own_ref[at + piece, 0:DK].astype(F32)
            other = other_ref[at + piece, 0:DK].astype(F32)
            buf[at + piece, 0:DK] = (own_weight * own + other_weight * other).astype(BF16)
            buf[at + piece, DK:ROWS] = aux
    for mask, out_ref in enumerate(outs):
        out_ref[...] = buf[chip ^ mask]


def join_call(own, other):
    return kernel_call(
        join_kernel,
        [("vmem", own), ("vmem", other)],
        [("vmem", own.shape[1:], BF16)] * OWNERS,
        [pltpu.VMEM(own.shape, BF16)],
        "join",
        0,
        4 << 20,
    )


def split_kernel(first_ref, *refs):
    records, (keep_ref, send_ref, enter_buf) = refs[:OWNERS], refs[OWNERS:]
    core, _, chip = place()
    second = core == 1
    for mask, record in enumerate(records):
        enter_buf[chip ^ mask] = record[...]
    for local in range(LOCAL):
        at = local * PIECES
        early = read_aux(enter_buf[at, DK:ROWS])
        before, after, joined = merge(early, read_aux(first_ref[at, DK:ROWS]))
        aux = aux_rows(*joined)
        plain = enter_buf[at, DK:ROWS]
        for piece in range(PIECES):
            chip_part = enter_buf[at + piece, 0:DK]
            moved = before * chip_part.astype(F32) + after * first_ref[at + piece, 0:DK].astype(F32)
            moved = moved.astype(BF16)
            keep_ref[at + piece, 0:DK] = jnp.where(second, moved, chip_part)
            send_ref[at + piece, 0:DK] = jnp.where(second, chip_part, moved)
            keep_ref[at + piece, DK:ROWS] = jnp.where(second, aux, plain)
            send_ref[at + piece, DK:ROWS] = jnp.where(second, plain, aux)


def split_call(records, first):
    shape = (OWNERS, ROWS, WIDTH)
    return kernel_call(
        split_kernel,
        [("vmem", first)] + [("vmem", record) for record in records],
        [("vmem", shape, BF16)] * 2,
        [pltpu.VMEM(shape, BF16)],
        "split",
        0,
        4 << 20,
    )


def near_kernel(
    heads, park, raw_hbm, key_hbm, rim_ref, tap_hbm, key_tap_hbm, val_hbm, rows_ref, *refs,
):
    count = len(heads)
    if park:
        own_ref, other_ref, act_ref = refs[:3]
        first_hbm = refs[6]
        refs = refs[3:6] + refs[7:]
    (
        query_hbm, num_hbm, stat_ref,
        raw_buf, raw_key_buf, key_buf, val_buf, query_buf, num_buf, tap_buf, sems,
    ) = refs
    places = [first_head(mine, 0) + local for mine, local in heads]
    taps_in = start_all(
        [
            pltpu.make_async_copy(tap_hbm, tap_buf.at[0], sems.at[5 * count]),
            pltpu.make_async_copy(key_tap_hbm, tap_buf.at[1], sems.at[5 * count + 1]),
        ]
    )
    if park:
        second = place()[0] == 1
        held = pltpu.make_async_copy(own_ref, first_hbm, sems.at[5 * count + 2])
        passed = pltpu.make_async_copy(other_ref, first_hbm, sems.at[5 * count + 2])

        @pl.when(second)
        def _():
            passed.start()

        @pl.when(jnp.logical_not(second))
        def _():
            held.start()

    coming, going = [], []
    for local in range(count):
        mid, wide = slice(local * DK, (local + 1) * DK), slice(local * DV, (local + 1) * DV)
        pairs = (
            (raw_hbm.at[:, span(places[local], DK)], raw_buf.at[local]),
            (key_hbm.at[:, span(places[local], DK)], raw_key_buf.at[local]),
            (val_hbm.at[:, span(places[local], DV)], val_buf.at[local]),
            (query_buf.at[local], query_hbm.at[:, mid]),
            (num_buf.at[local], num_hbm.at[:, wide]),
        )
        copies = [pltpu.make_async_copy(a, b, sems.at[5 * local + k]) for k, (a, b) in enumerate(pairs)]
        held_key = park and heads[local][0]
        coming.append(start_all(copies[:1] + copies[2:3] if held_key else copies[:3]))
        going.append(copies[3:])
    for copy in taps_in:
        copy.wait()
    causal = lax.broadcasted_iota(jnp.int32, (TILE, TILE), 0) >= lax.broadcasted_iota(
        jnp.int32, (TILE, TILE), 1
    )
    for local in range(count):
        head = places[local]
        coming[local][0].wait()
        columns, rim_columns = span(head, DK), span(HEADS + head, DK)
        for start, act in conv_rows(columns, rim_columns, raw_buf[local], rim_ref, tap_buf.at[0]):
            query_buf[local, start : start + STEP] = act
        going[local][0].start()
        if park and heads[local][0]:
            key_act = act_ref.at[:, (local * DK) : (local + 1) * DK]
        else:
            coming[local][1].wait()
            for start, act in conv_rows(columns, columns, raw_key_buf[local], rim_ref, tap_buf.at[1]):
                key_buf[local, start : start + STEP] = act
            key_act = key_buf.at[local]
        coming[local][-1].wait()
        peak = row_of(rows_ref, 1, head)
        level = row_of(rows_ref, 0, head)
        peak_column = column(peak)
        scores = {
            s: lax.dot_general(query_buf[local, s:BLK], key_act[s : s + TILE], NT, preferred_element_type=F32)
            for s in range(0, BLK, TILE)
        }
        for t in range(0, BLK, TILE):
            rows_peak = widen(peak_column[t : t + TILE], TILE)
            parts = []
            for s in range(0, t + TILE, TILE):
                exponent = level[:, s : s + TILE] - rows_peak
                if s == t:
                    exponent = jnp.where(causal, exponent, -jnp.inf)
                parts.append((scores[s][t - s : t - s + TILE] * (SCALE * jnp.exp(exponent))).astype(BF16))
            mixing = jnp.concatenate(parts, axis=1)
            num = jnp.dot(mixing, val_buf[local, 0 : t + TILE], preferred_element_type=F32)
            num_buf[local, t : t + TILE] = num.astype(NUM)
            added = sum(part.astype(F32) for part in parts)
            den = jnp.sum(added[:, 0:128] + added[:, 128:TILE], axis=1, keepdims=True)
            stat_ref[local, 0:1, t : t + TILE] = jnp.broadcast_to(den, (TILE, 128)).T[0:1]
        stat_ref[local, 1:2] = peak
        stat_ref[local, 2:8] = jnp.zeros((6, BLK), F32)
        going[local][1].start()
    for copies in going:
        for copy in copies:
            copy.wait()
    if park:
        held.wait()


def near_call(heads, query_raw, key_raw, rim, query_conv, key_conv, values, rows, parked=()):
    count = len(heads)
    inputs = [
        ("hbm", query_raw), ("hbm", key_raw), ("vmem", rim), ("hbm", query_conv), ("hbm", key_conv),
        ("hbm", values), ("vmem", rows),
    ]
    outputs = [
        ("hbm", (BLK, count * DK), BF16),
        ("hbm", (BLK, count * DV), NUM),
        ("vmem", (count, 8, BLK), F32),
    ]
    if parked:
        inputs += [("vmem", record) for record in parked]
        outputs += [("hbm", parked[0].shape, BF16)]
    return kernel_call(
        functools.partial(near_kernel, heads, bool(parked)),
        inputs,
        outputs,
        [
            pltpu.VMEM((count, BLK, DK), BF16),
            pltpu.VMEM((count, BLK, DK), BF16),
            pltpu.VMEM((count, BLK, DK), BF16),
            pltpu.VMEM((count, BLK, DV), BF16),
            pltpu.VMEM((count, BLK, DK), BF16),
            pltpu.VMEM((count, BLK, DV), NUM),
            pltpu.VMEM((2, TAPS, HEADS * DK), BF16),
            pltpu.SemaphoreType.DMA((5 * count + 3,)),
        ],
        "near",
        count * 2 * BLK * BLK * (DK + DV),
        count * 5 << 20,
    )


def total_kernel(rule, *refs):
    records, (stack_ref, out_ref) = refs[:-2], refs[-2:]
    _, cube, chip = place()
    count = len(records)
    for mask, record in enumerate(records):
        stack_ref[mask if rule else chip ^ mask] = record[...]
    norms, tops, decays = [], [], []
    for k in range(count):
        norm, top, decay = read_aux(stack_ref[k, DK:ROWS])
        norms.append(norm)
        tops.append(jnp.where(cube > rule[k], top, EMPTY) if rule else top)
        decays.append(decay)
    after = jnp.zeros((1, WIDTH), F32)
    logs = [None] * count
    for k in reversed(range(count)):
        logs[k] = tops[k] + after
        after = after + decays[k]
    peak = functools.reduce(jnp.maximum, logs)
    weights = [jnp.exp(log - peak) for log in logs]
    joined = [sum(w * n[part] for w, n in zip(weights, norms)) for part in range(SPLIT)]
    for start in range(0, DK, STEP):
        acc = weights[0] * stack_ref[0, start : start + STEP].astype(F32)
        for k in range(1, count):
            acc = acc + weights[k] * stack_ref[k, start : start + STEP].astype(F32)
        out_ref[start : start + STEP] = acc.astype(BF16)
    out_ref[DK:ROWS] = aux_rows(joined, peak, after)


def total_call(records, rule=None):
    return kernel_call(
        functools.partial(total_kernel, rule),
        [("vmem", record) for record in records],
        [("vmem", (len(records), ROWS, WIDTH), BF16), ("vmem", (ROWS, WIDTH), BF16)],
        [],
        "total",
        0,
        1 << 20,
    )


def prefix_kernel(rec_ref, enter_ref, *refs):
    outs, buf = refs[:-1], refs[-1]
    _, cube, chip = place()
    norms, top, _ = read_aux(enter_ref[DK:ROWS])
    state = (norms, jnp.where(cube > 0, top, EMPTY), jnp.zeros((1, WIDTH), F32))
    weights = []
    for k in range(OWNERS):
        buf[k, DK:ROWS] = aux_rows(*state)
        if k + 1 < OWNERS:
            early, late, state = merge(state, read_aux(rec_ref[k, DK:ROWS]))
            weights.append((early, late))
    for start in range(0, DK, STEP):
        run = enter_ref[start : start + STEP].astype(F32)
        for k in range(OWNERS):
            buf[k, start : start + STEP] = run.astype(BF16)
            if k + 1 < OWNERS:
                early, late = weights[k]
                run = early * run + late * rec_ref[k, start : start + STEP].astype(F32)
    for mask, out_ref in enumerate(outs):
        out_ref[...] = buf[chip ^ mask]


def prefix_call(records, entering):
    return kernel_call(
        prefix_kernel,
        [("vmem", records), ("vmem", entering)],
        [("vmem", (ROWS, WIDTH), BF16)] * OWNERS,
        [pltpu.VMEM(records.shape, BF16)],
        "prefix",
        0,
        2 << 20,
    )


def far_kernel(mine, slots, sources, *refs):
    near, enter_ref, (out_ref, ready, sems) = refs[: 3 * sources], refs[3 * sources], refs[-3:]
    copies = []
    for local, (source, slot) in enumerate(slots):
        query_ref, num_ref, stat_ref = near[3 * source : 3 * source + 3]
        mid, wide = slice(slot * DK, (slot + 1) * DK), slice(slot * DV, (slot + 1) * DV)
        at = local * PIECES
        aux = enter_ref[at, DK:ROWS]
        _, far_log, _ = read_aux(aux)
        far_log = far_log[:, 0:1]
        query = query_ref[:, mid]
        den = stat_ref[slot, 0:1]
        near_peak = stat_ref[slot, 1:2]
        peak = jnp.maximum(near_peak, far_log)
        near_part = jnp.exp(near_peak - peak)
        far_part = jnp.exp(far_log - peak) * SCALE
        below = near_part * den + far_part * dot_norm(aux, query)
        scale = 1.0 / jnp.maximum(jnp.abs(below), 1.0)
        near_column = column(near_part * scale)
        far_column = column(far_part * scale)
        memory = jnp.concatenate([enter_ref[at + piece, 0:DK] for piece in range(PIECES)], axis=1)
        for t in range(0, BLK, TILE):
            far = jnp.dot(query[t : t + TILE], memory, preferred_element_type=F32)
            near_weight = widen(near_column[t : t + TILE], DV)
            far_weight = widen(far_column[t : t + TILE], DV)
            near_rows = num_ref[t : t + TILE, wide].astype(F32)
            ready[local, t : t + TILE] = (near_weight * near_rows + far_weight * far).astype(BF16)
        head = first_head(mine, 0) + local
        copies.append(pltpu.make_async_copy(ready.at[local], out_ref.at[:, span(head, DV)], sems.at[local]))
        copies[-1].start()
    for copy in copies:
        copy.wait()


def far_call(mine, near, entering, out=None):
    slots, operands = [], []
    for source, (heads, results) in enumerate(near):
        operands += results
        slots += [(local, (source, slot)) for slot, (side, local) in enumerate(heads) if side == mine]
    slots = [slot for _, slot in sorted(slots)]
    operands = [pltpu.with_memory_space_constraint(x, pltpu.VMEM) for x in operands + [entering]]
    in_specs = [VMEM_SPEC] * len(operands)
    aliases = {}
    if out is not None:
        in_specs.append(pl.BlockSpec(memory_space=pltpu.HBM))
        aliases = {len(operands): 0}
        operands.append(out)
    return pl.pallas_call(
        functools.partial(far_kernel, mine, slots, len(near)),
        in_specs=in_specs,
        out_specs=pl.BlockSpec(memory_space=pltpu.HBM),
        out_shape=jax.ShapeDtypeStruct((BLK, HEADS * DV), BF16),
        scratch_shapes=[pltpu.VMEM((LOCAL, BLK, DV), BF16), pltpu.SemaphoreType.DMA((LOCAL,))],
        input_output_aliases=aliases,
        compiler_params=pltpu.CompilerParams(vmem_limit_bytes=8 << 20),
        name="far",
        cost_estimate=pl.CostEstimate(
            flops=LOCAL * 2 * BLK * DK * DV, transcendentals=0, bytes_accessed=LOCAL * 5 << 20
        ),
    )(*operands)


def on_device(query_raw, key_raw, values, in_gate, forget_gate, query_conv, key_conv):
    devices = lax.axis_size(AXES)
    cube_size = 2 * OWNERS
    cubes = devices // cube_size
    line = [(i, i + 1) for i in range(devices - 1)]
    swap = [(i, i ^ 1) for i in range(devices)]
    up = lambda distance: [(i, i + distance * cube_size) for i in range(devices - distance * cube_size)]
    after = lambda x, *done: lax.optimization_barrier((x,) + done)[0]

    def spread(records):
        moved = {0: records[0]}
        for mask in ORDER:
            route = [(i, i ^ (2 * mask)) for i in range(devices)]
            moved[mask] = lax.ppermute(records[mask], AXES, route)
        return [moved[mask] for mask in range(OWNERS)]

    rim = lax.ppermute(tails_call(key_raw, query_raw), AXES, line)
    rows, key_held, taps_held, val_held = prepare_call(in_gate, forget_gate, key_raw, key_conv, values)
    near_args = (query_raw, key_raw, rim, query_conv, key_conv, values)

    late = late_state_call(key_held, taps_held, val_held, rows)
    sent = early_state_call(key_held, rim, taps_held, val_held, rows, *late)
    rows = after(rows, sent)
    other = lax.ppermute(sent, AXES, swap)
    own, key_act = state_call(key_held, rim, taps_held, val_held, rows)
    joined = join_call(own, other)
    rows = after(rows, joined[0])
    records = spread(joined)
    *near_first, first = near_call(PARTS[0], *near_args, rows, (own, other, key_act))
    records[0] = after(records[0], near_first[0])
    stack, total = total_call(records)
    rows = after(rows, total)
    entering = lax.ppermute(total, AXES, up(1))
    distance = 1
    while distance < cubes - 1:
        earlier = lax.ppermute(entering, AXES, up(distance))
        entering = total_call([earlier, entering], (distance, 0))[1]
        distance *= 2
    near_second = near_call(PARTS[1], *near_args, rows)
    before = prefix_call(after(stack, near_second[0]), entering)
    rows = after(rows, before[0])
    records = spread(before)
    near_third = near_call(PARTS[2], *near_args, rows)
    records[0] = after(records[0], near_third[0])
    keep, send = split_call(records, first)
    enter_theirs = lax.ppermute(send, AXES, swap)
    near = list(zip(PARTS, ([*near_first], [*near_second], [*near_third])))
    sides = [[part for part in near if any(side == mine for side, _ in part[0])] for mine in (True, False)]
    out = far_call(True, sides[0], keep)
    return far_call(False, sides[1], enter_theirs, out)


def solution(mesh):
    split = P(AXES, None)
    in_specs = (split, split, split, split, split, P(), P())
    return jax.shard_map(on_device, mesh=mesh, in_specs=in_specs, out_specs=split, check_vma=False)
```

```python
import functools

import jax
import jax.numpy as jnp
from jax import lax
from jax.experimental import pallas as pl
from jax.experimental.pallas import tpu as pltpu
from jax.sharding import PartitionSpec as P

AXES = ("ctx", "head")
HEADS = 8
CHAINS = 1
GROUP = HEADS // 2
LOCAL = GROUP // CHAINS
OWNERS = 8
DK = 256
DV = 512
WIDTH = LOCAL * DV // OWNERS
PIECES = DV // WIDTH
SPLIT = DK // WIDTH
AUX = 8
RIM = 8
EARLY = 16
ROWS = DK + AUX
BLK = 512
TAPS = 4
TILE = 256
STEP = 128
EMPTY = -1e30
ORDER = (1, 7, 2, 6, 4, 5, 3)
SIDES = [(True, local) for local in range(LOCAL)] + [(False, local) for local in range(LOCAL)]
PARTS = (SIDES[:5], SIDES[5:6], SIDES[6:])
SCALE = DK**-0.5
F32 = jnp.float32
BF16 = jnp.bfloat16
NUM = BF16
NT = (((1,), (1,)), ((), ()))


def narrow(x):
    return x.astype(BF16).astype(F32)


def split3(x):
    top = narrow(x)
    middle = narrow(x - top)
    return [top, middle, x - top - middle]


def aux_rows(norms, top, decay):
    parts = []
    for norm in norms:
        high = narrow(norm)
        parts += [high, norm - high]
    parts += split3(top) + split3(decay)
    row = lax.broadcasted_iota(jnp.int32, (AUX, WIDTH), 0)
    out = jnp.zeros((AUX, WIDTH), F32)
    for index, part in enumerate(parts):
        out = jnp.where(row == index, part, out)
    return out.astype(BF16)


def read_aux(aux):
    aux = aux.astype(F32)
    norms = [aux[2 * k : 2 * k + 1] + aux[2 * k + 1 : 2 * k + 2] for k in range(SPLIT)]
    at = 2 * SPLIT
    top = aux[at : at + 1] + aux[at + 1 : at + 2] + aux[at + 2 : at + 3]
    decay = aux[at + 3 : at + 4] + aux[at + 4 : at + 5] + aux[at + 5 : at + 6]
    return norms, top, decay


def dot_norm(aux, query):
    out = None
    for k in range(SPLIT):
        part = lax.dot_general(
            aux, query[:, k * WIDTH : (k + 1) * WIDTH], NT, preferred_element_type=F32
        )
        part = part[2 * k : 2 * k + 1] + part[2 * k + 1 : 2 * k + 2]
        out = part if out is None else out + part
    return out


def column(row):
    return jnp.broadcast_to(row, (128, row.shape[1])).T


def widen(col, width):
    return jnp.concatenate([col] * (width // 128), axis=1)


def place():
    me = lax.axis_index("ctx") * lax.axis_size("head") + lax.axis_index("head")
    return me % 2, me // (2 * OWNERS), me % (2 * OWNERS) // 2


def first_head(mine, chain):
    core = place()[0]
    return GROUP * (core if mine else 1 - core) + LOCAL * chain


def span(index, width):
    return pl.ds(pl.multiple_of(index * width, width), width)


VMEM_SPEC = pl.BlockSpec(memory_space=pltpu.VMEM)


def tails_kernel(key_hbm, query_hbm, out_ref, sems):
    width = key_hbm.shape[1]
    last = pl.ds(BLK - RIM, RIM)
    for copy in start_all(
        [
            pltpu.make_async_copy(key_hbm.at[last], out_ref.at[:, 0:width], sems.at[0]),
            pltpu.make_async_copy(query_hbm.at[last], out_ref.at[:, width : 2 * width], sems.at[1]),
        ]
    ):
        copy.wait()


def tails_call(key_raw, query_raw):
    return kernel_call(
        tails_kernel,
        [("hbm", key_raw), ("hbm", query_raw)],
        [("vmem", (RIM, 2 * key_raw.shape[1]), BF16)],
        [pltpu.SemaphoreType.DMA((2,))],
        "tails",
        0,
        1 << 17,
    )[0]


def prepare_kernel(in_hbm, forget_hbm, key_hbm, tap_hbm, val_hbm, rows_ref, key_ref, tap_ref, val_ref, gate_buf, sems):
    gates_in = start_all(
        [
            pltpu.make_async_copy(in_hbm, gate_buf.at[0], sems.at[0]),
            pltpu.make_async_copy(forget_hbm, gate_buf.at[1], sems.at[1]),
        ]
    )
    loads = start_all(
        [
            pltpu.make_async_copy(key_hbm, key_ref, sems.at[2]),
            pltpu.make_async_copy(tap_hbm, tap_ref, sems.at[3]),
            pltpu.make_async_copy(val_hbm, val_ref, sems.at[4]),
        ]
    )
    for copy in gates_in:
        copy.wait()
    gate = gate_buf[0].astype(F32)
    forget = gate_buf[1].astype(F32)
    log_forget = jnp.minimum(forget, 0.0) - jnp.log1p(jnp.exp(-jnp.abs(forget)))
    lane = lax.broadcasted_iota(jnp.int32, (HEADS, BLK), 1)
    total = log_forget
    shift = 1
    while shift < BLK:
        total = total + jnp.where(lane >= shift, pltpu.roll(total, shift, 1), 0.0)
        shift *= 2
    level = gate - total
    top = level
    shift = 1
    while shift < BLK:
        top = jnp.maximum(top, jnp.where(lane >= shift, pltpu.roll(top, shift, 1), -jnp.inf))
        shift *= 2
    last_top = top[:, BLK - 1 :]
    last_total = total[:, BLK - 1 :]
    out = (
        level,
        top,
        jnp.exp(level - last_top),
        jnp.broadcast_to(last_total + last_top, (HEADS, BLK)),
        jnp.broadcast_to(last_total, (HEADS, BLK)),
    )
    for index, part in enumerate(out):
        rows_ref[index * HEADS : (index + 1) * HEADS] = part
    for copy in loads:
        copy.wait()


def prepare_call(in_gate, forget_gate, key_raw, key_conv, values):
    return kernel_call(
        prepare_kernel,
        [("hbm", in_gate.T), ("hbm", forget_gate.T), ("hbm", key_raw), ("hbm", key_conv), ("hbm", values)],
        [
            ("vmem", (5 * HEADS, BLK), F32),
            ("vmem", key_raw.shape, BF16),
            ("vmem", key_conv.shape, BF16),
            ("vmem", values.shape, BF16),
        ],
        [pltpu.VMEM((2, HEADS, BLK), BF16), pltpu.SemaphoreType.DMA((5,))],
        "prepare",
        0,
        6 << 20,
    )


def row_of(rows_ref, kind, head):
    return rows_ref[pl.ds(kind * HEADS + head, 1), :]


HBM_SPEC = pl.BlockSpec(memory_space=pltpu.HBM)
LIMIT = 20 << 20


def kernel_call(kernel, inputs, outputs, scratch, name, flops, size):
    in_specs, operands = [], []
    for where, x in inputs:
        operands.append(pltpu.with_memory_space_constraint(x, pltpu.VMEM if where == "vmem" else pltpu.HBM))
        in_specs.append(VMEM_SPEC if where == "vmem" else HBM_SPEC)
    return pl.pallas_call(
        kernel,
        in_specs=in_specs,
        out_specs=[VMEM_SPEC if where == "vmem" else HBM_SPEC for where, _, _ in outputs],
        out_shape=[
            (pltpu.VMEM if where == "vmem" else pltpu.HBM)(shape, dtype)
            for where, shape, dtype in outputs
        ],
        scratch_shapes=scratch,
        name=name,
        cost_estimate=pl.CostEstimate(flops=flops, transcendentals=0, bytes_accessed=size),
        compiler_params=pltpu.CompilerParams(vmem_limit_bytes=LIMIT),
    )(*operands)


def conv_rows(columns, rim_columns, raw, rim_ref, tap_ref):
    taps = 0.5 * tap_ref[:, columns].astype(F32)
    earlier = rim_ref[:, rim_columns].astype(F32)
    for start in range(0, BLK, STEP):
        here = raw[start : start + STEP].astype(F32)
        wide = jnp.concatenate([earlier, here], axis=0)
        first = 8 - (TAPS - 1)
        mixed = taps[0:1] * wide[first : first + STEP]
        for tap in range(1, TAPS):
            mixed = mixed + taps[tap : tap + 1] * wide[first + tap : first + tap + STEP]
        earlier = here[STEP - 8 :]
        yield start, (mixed * (jnp.tanh(mixed) + 1.0)).astype(BF16)


def start_all(copies):
    for copy in copies:
        copy.start()
    return copies


def write_record(rec_ref, local, memory, norm, top, decay):
    aux = aux_rows([norm[:, k * WIDTH : (k + 1) * WIDTH] for k in range(SPLIT)], top, decay)
    for piece in range(PIECES):
        at = local * PIECES + piece
        rec_ref[at, 0:DK] = memory[:, piece * WIDTH : (piece + 1) * WIDTH].astype(BF16)
        rec_ref[at, DK:ROWS] = aux


def outer(weighted, values):
    return lax.dot_general(weighted, values, (((0,), (0,)), ((), ())), preferred_element_type=F32)


def state_kernel(raw_ref, rim_ref, tap_ref, val_ref, rows_ref, rec_ref, act_ref, weighted):
    for local in range(LOCAL):
        head = first_head(True, 0) + local
        weight = column(row_of(rows_ref, 2, head))
        norm = jnp.zeros((1, DK), F32)
        columns = span(head, DK)
        for start, act in conv_rows(columns, columns, raw_ref[:, columns], rim_ref, tap_ref):
            act_ref[start : start + STEP, local * DK : (local + 1) * DK] = act
            scaled = act.astype(F32) * widen(weight[start : start + STEP], DK)
            norm = norm + jnp.sum(scaled, axis=0, keepdims=True)
            weighted[local % 2, start : start + STEP] = scaled.astype(BF16)
        memory = outer(weighted[local % 2], val_ref[:, span(head, DV)])
        top = row_of(rows_ref, 3, head)[:, :WIDTH]
        decay = row_of(rows_ref, 4, head)[:, :WIDTH]
        write_record(rec_ref, local, memory, norm, top, decay)


def state_call(raw, rim, taps, values, rows):
    return kernel_call(
        state_kernel,
        [("vmem", raw), ("vmem", rim), ("vmem", taps), ("vmem", values), ("vmem", rows)],
        [("vmem", (OWNERS, ROWS, WIDTH), BF16), ("vmem", (BLK, LOCAL * DK), BF16)],
        [pltpu.VMEM((2, BLK, DK), BF16)],
        "state",
        LOCAL * 2 * BLK * DK * DV,
        LOCAL * 3 << 20,
    )


def late_state_kernel(raw_ref, tap_ref, val_ref, rows_ref, memory_ref, norm_ref, no_rim, weighted):
    no_rim[...] = jnp.zeros((RIM, HEADS * DK), BF16)
    lanes = lax.broadcasted_iota(jnp.int32, (1, BLK), 1)
    for local in range(LOCAL):
        head = first_head(False, 0) + local
        weight = column(jnp.where(lanes >= EARLY, row_of(rows_ref, 2, head), 0.0))
        norm = jnp.zeros((1, DK), F32)
        columns = span(head, DK)
        for start, act in conv_rows(columns, columns, raw_ref[:, columns], no_rim, tap_ref):
            scaled = act.astype(F32) * widen(weight[start : start + STEP], DK)
            norm = norm + jnp.sum(scaled, axis=0, keepdims=True)
            weighted[local % 2, start : start + STEP] = scaled.astype(BF16)
        memory_ref[local] = outer(weighted[local % 2], val_ref[:, span(head, DV)])
        norm_ref[local] = jnp.broadcast_to(norm, (8, DK))


def late_state_call(raw, taps, values, rows):
    return kernel_call(
        late_state_kernel,
        [("vmem", raw), ("vmem", taps), ("vmem", values), ("vmem", rows)],
        [("vmem", (LOCAL, DK, DV), F32), ("vmem", (LOCAL, 8, DK), F32)],
        [
            pltpu.VMEM((RIM, HEADS * DK), BF16),
            pltpu.VMEM((2, BLK, DK), BF16),
        ],
        "late_state",
        LOCAL * 2 * BLK * DK * DV,
        LOCAL * 3 << 20,
    )


def early_state_kernel(raw_ref, rim_ref, tap_ref, val_ref, rows_ref, memory_ref, norm_ref, rec_ref, padded):
    for local in range(LOCAL):
        head = first_head(False, 0) + local
        columns = span(head, DK)
        weight = column(row_of(rows_ref, 2, head)[:, 0:128])[0:EARLY]
        padded[local, 0:8] = rim_ref[:, columns].astype(F32)
        padded[local, 8 : 8 + EARLY] = raw_ref[0:EARLY, columns].astype(F32)
        taps = 0.5 * tap_ref[:, columns].astype(F32)
        first = 8 - (TAPS - 1)
        mixed = taps[0:1] * padded[local, first : first + EARLY]
        for tap in range(1, TAPS):
            mixed = mixed + taps[tap : tap + 1] * padded[local, first + tap : first + tap + EARLY]
        act = (mixed * (jnp.tanh(mixed) + 1.0)).astype(BF16)
        scaled = act.astype(F32) * widen(weight, DK)
        norm = norm_ref[local, 0:1] + jnp.sum(scaled, axis=0, keepdims=True)
        memory = memory_ref[local] + outer(scaled.astype(BF16), val_ref[0:EARLY, span(head, DV)])
        top = row_of(rows_ref, 3, head)[:, :WIDTH]
        decay = row_of(rows_ref, 4, head)[:, :WIDTH]
        write_record(rec_ref, local, memory, norm, top, decay)


def early_state_call(raw, rim, taps, values, rows, memory, norm):
    return kernel_call(
        early_state_kernel,
        [("vmem", x) for x in (raw, rim, taps, values, rows, memory, norm)],
        [("vmem", (OWNERS, ROWS, WIDTH), BF16)],
        [pltpu.VMEM((LOCAL, 8 + EARLY, DK), F32)],
        "early_state",
        1 << 20,
        4 << 20,
    )[0]


def merge(early, late):
    norms, top, decay = early
    later_norms, later_top, later_decay = late
    joined_top = jnp.maximum(top + later_decay, later_top)
    before = jnp.exp(top + later_decay - joined_top)
    after = jnp.exp(later_top - joined_top)
    joined = [before * a + after * b for a, b in zip(norms, later_norms)]
    return before, after, (joined, joined_top, decay + later_decay)


def join_kernel(own_ref, other_ref, *refs):
    outs, buf = refs[:-1], refs[-1]
    core, _, chip = place()
    second = core == 1
    for local in range(LOCAL):
        at = local * PIECES
        norms, top, decay = read_aux(own_ref[at, DK:ROWS])
        other_norms, other_top, other_decay = read_aux(other_ref[at, DK:ROWS])
        own_log = top + jnp.where(second, 0.0, other_decay)
        other_log = other_top + jnp.where(second, decay, 0.0)
        joined_top = jnp.maximum(own_log, other_log)
        own_weight = jnp.exp(own_log - joined_top)
        other_weight = jnp.exp(other_log - joined_top)
        joined = [own_weight * a + other_weight * b for a, b in zip(norms, other_norms)]
        aux = aux_rows(joined, joined_top, decay + other_decay)
        for piece in range(PIECES):
            own = own_ref[at + piece, 0:DK].astype(F32)
            other = other_ref[at + piece, 0:DK].astype(F32)
            buf[at + piece, 0:DK] = (own_weight * own + other_weight * other).astype(BF16)
            buf[at + piece, DK:ROWS] = aux
    for mask, out_ref in enumerate(outs):
        out_ref[...] = buf[chip ^ mask]


def join_call(own, other):
    return kernel_call(
        join_kernel,
        [("vmem", own), ("vmem", other)],
        [("vmem", own.shape[1:], BF16)] * OWNERS,
        [pltpu.VMEM(own.shape, BF16)],
        "join",
        0,
        4 << 20,
    )


def split_kernel(first_ref, *refs):
    records, (keep_ref, send_ref) = refs[:OWNERS], refs[OWNERS:]
    core, _, chip = place()
    second = core == 1
    for mask, record in enumerate(records):
        at = chip ^ mask
        before, after, joined = merge(read_aux(record[DK:ROWS]), read_aux(first_ref[at, DK:ROWS]))
        aux = aux_rows(*joined)
        plain = record[DK:ROWS]
        keep_ref[at, DK:ROWS] = jnp.where(second, aux, plain)
        send_ref[at, DK:ROWS] = jnp.where(second, plain, aux)
        for start in range(0, DK, STEP):
            chip_part = record[start : start + STEP]
            first_part = first_ref[at, start : start + STEP]
            moved = (before * chip_part.astype(F32) + after * first_part.astype(F32)).astype(BF16)
            keep_ref[at, start : start + STEP] = jnp.where(second, moved, chip_part)
            send_ref[at, start : start + STEP] = jnp.where(second, chip_part, moved)


def split_call(records, first):
    shape = (OWNERS, ROWS, WIDTH)
    return kernel_call(
        split_kernel,
        [("vmem", first)] + [("vmem", record) for record in records],
        [("vmem", shape, BF16)] * 2,
        [],
        "split",
        0,
        4 << 20,
    )


def near_kernel(
    heads, park, raw_hbm, key_hbm, rim_ref, tap_hbm, key_tap_hbm, val_hbm, rows_ref, *refs,
):
    count = len(heads)
    if park:
        own_ref, other_ref, act_ref = refs[:3]
        first_hbm = refs[6]
        refs = refs[3:6] + refs[7:]
    (
        query_hbm, num_hbm, stat_ref,
        raw_buf, raw_key_buf, key_buf, val_buf, query_buf, num_buf, tap_buf, sems,
    ) = refs
    places = [first_head(mine, 0) + local for mine, local in heads]
    taps_in = start_all(
        [
            pltpu.make_async_copy(tap_hbm, tap_buf.at[0], sems.at[5 * count]),
            pltpu.make_async_copy(key_tap_hbm, tap_buf.at[1], sems.at[5 * count + 1]),
        ]
    )
    if park:
        second = place()[0] == 1
        held = pltpu.make_async_copy(own_ref, first_hbm, sems.at[5 * count + 2])
        passed = pltpu.make_async_copy(other_ref, first_hbm, sems.at[5 * count + 2])

        @pl.when(second)
        def _():
            passed.start()

        @pl.when(jnp.logical_not(second))
        def _():
            held.start()

    coming, going = [], []
    for local in range(count):
        mid, wide = slice(local * DK, (local + 1) * DK), slice(local * DV, (local + 1) * DV)
        pairs = (
            (raw_hbm.at[:, span(places[local], DK)], raw_buf.at[local]),
            (key_hbm.at[:, span(places[local], DK)], raw_key_buf.at[local]),
            (val_hbm.at[:, span(places[local], DV)], val_buf.at[local]),
            (query_buf.at[local], query_hbm.at[:, mid]),
            (num_buf.at[local], num_hbm.at[:, wide]),
        )
        copies = [pltpu.make_async_copy(a, b, sems.at[5 * local + k]) for k, (a, b) in enumerate(pairs)]
        held_key = park and heads[local][0]
        coming.append(start_all(copies[:1] + copies[2:3] if held_key else copies[:3]))
        going.append(copies[3:])
    for copy in taps_in:
        copy.wait()
    causal = lax.broadcasted_iota(jnp.int32, (TILE, TILE), 0) >= lax.broadcasted_iota(
        jnp.int32, (TILE, TILE), 1
    )
    for local in range(count):
        head = places[local]
        coming[local][0].wait()
        columns, rim_columns = span(head, DK), span(HEADS + head, DK)
        for start, act in conv_rows(columns, rim_columns, raw_buf[local], rim_ref, tap_buf.at[0]):
            query_buf[local, start : start + STEP] = act
        going[local][0].start()
        if park and heads[local][0]:
            key_act = act_ref.at[:, (local * DK) : (local + 1) * DK]
        else:
            coming[local][1].wait()
            for start, act in conv_rows(columns, columns, raw_key_buf[local], rim_ref, tap_buf.at[1]):
                key_buf[local, start : start + STEP] = act
            key_act = key_buf.at[local]
        coming[local][-1].wait()
        peak = row_of(rows_ref, 1, head)
        level = row_of(rows_ref, 0, head)
        peak_column = column(peak)
        scores = {
            s: lax.dot_general(query_buf[local, s:BLK], key_act[s : s + TILE], NT, preferred_element_type=F32)
            for s in range(0, BLK, TILE)
        }
        for t in range(0, BLK, TILE):
            rows_peak = widen(peak_column[t : t + TILE], TILE)
            parts = []
            for s in range(0, t + TILE, TILE):
                exponent = level[:, s : s + TILE] - rows_peak
                if s == t:
                    exponent = jnp.where(causal, exponent, -jnp.inf)
                parts.append((scores[s][t - s : t - s + TILE] * (SCALE * jnp.exp(exponent))).astype(BF16))
            mixing = jnp.concatenate(parts, axis=1)
            num = jnp.dot(mixing, val_buf[local, 0 : t + TILE], preferred_element_type=F32)
            num_buf[local, t : t + TILE] = num.astype(NUM)
            added = sum(part.astype(F32) for part in parts)
            den = jnp.sum(added[:, 0:128] + added[:, 128:TILE], axis=1, keepdims=True)
            stat_ref[local, 0:1, t : t + TILE] = jnp.broadcast_to(den, (TILE, 128)).T[0:1]
        stat_ref[local, 1:2] = peak
        stat_ref[local, 2:8] = jnp.zeros((6, BLK), F32)
        going[local][1].start()
    for copies in going:
        for copy in copies:
            copy.wait()
    if park:
        held.wait()


def near_call(heads, query_raw, key_raw, rim, query_conv, key_conv, values, rows, parked=()):
    count = len(heads)
    inputs = [
        ("hbm", query_raw), ("hbm", key_raw), ("vmem", rim), ("hbm", query_conv), ("hbm", key_conv),
        ("hbm", values), ("vmem", rows),
    ]
    outputs = [
        ("hbm", (BLK, count * DK), BF16),
        ("hbm", (BLK, count * DV), NUM),
        ("vmem", (count, 8, BLK), F32),
    ]
    if parked:
        inputs += [("vmem", record) for record in parked]
        outputs += [("hbm", parked[0].shape, BF16)]
    return kernel_call(
        functools.partial(near_kernel, heads, bool(parked)),
        inputs,
        outputs,
        [
            pltpu.VMEM((count, BLK, DK), BF16),
            pltpu.VMEM((count, BLK, DK), BF16),
            pltpu.VMEM((count, BLK, DK), BF16),
            pltpu.VMEM((count, BLK, DV), BF16),
            pltpu.VMEM((count, BLK, DK), BF16),
            pltpu.VMEM((count, BLK, DV), NUM),
            pltpu.VMEM((2, TAPS, HEADS * DK), BF16),
            pltpu.SemaphoreType.DMA((5 * count + 3,)),
        ],
        "near",
        count * 2 * BLK * BLK * (DK + DV),
        count * 5 << 20,
    )


def total_kernel(rule, *refs):
    records, (stack_ref, out_ref) = refs[:-2], refs[-2:]
    _, cube, chip = place()
    count = len(records)
    for mask, record in enumerate(records):
        stack_ref[mask if rule else chip ^ mask] = record[...]
    norms, tops, decays = [], [], []
    for k in range(count):
        norm, top, decay = read_aux(stack_ref[k, DK:ROWS])
        norms.append(norm)
        tops.append(jnp.where(cube > rule[k], top, EMPTY) if rule else top)
        decays.append(decay)
    after = jnp.zeros((1, WIDTH), F32)
    logs = [None] * count
    for k in reversed(range(count)):
        logs[k] = tops[k] + after
        after = after + decays[k]
    peak = functools.reduce(jnp.maximum, logs)
    weights = [jnp.exp(log - peak) for log in logs]
    joined = [sum(w * n[part] for w, n in zip(weights, norms)) for part in range(SPLIT)]
    for start in range(0, DK, STEP):
        acc = weights[0] * stack_ref[0, start : start + STEP].astype(F32)
        for k in range(1, count):
            acc = acc + weights[k] * stack_ref[k, start : start + STEP].astype(F32)
        out_ref[start : start + STEP] = acc.astype(BF16)
    out_ref[DK:ROWS] = aux_rows(joined, peak, after)


def total_call(records, rule=None):
    return kernel_call(
        functools.partial(total_kernel, rule),
        [("vmem", record) for record in records],
        [("vmem", (len(records), ROWS, WIDTH), BF16), ("vmem", (ROWS, WIDTH), BF16)],
        [],
        "total",
        0,
        1 << 20,
    )


def prefix_kernel(rec_ref, enter_ref, *refs):
    outs, buf = refs[:-1], refs[-1]
    _, cube, chip = place()
    norms, top, _ = read_aux(enter_ref[DK:ROWS])
    state = (norms, jnp.where(cube > 0, top, EMPTY), jnp.zeros((1, WIDTH), F32))
    weights = []
    for k in range(OWNERS):
        buf[k, DK:ROWS] = aux_rows(*state)
        if k + 1 < OWNERS:
            early, late, state = merge(state, read_aux(rec_ref[k, DK:ROWS]))
            weights.append((early, late))
    for start in range(0, DK, STEP):
        run = enter_ref[start : start + STEP].astype(F32)
        for k in range(OWNERS):
            buf[k, start : start + STEP] = run.astype(BF16)
            if k + 1 < OWNERS:
                early, late = weights[k]
                run = early * run + late * rec_ref[k, start : start + STEP].astype(F32)
    for mask, out_ref in enumerate(outs):
        out_ref[...] = buf[chip ^ mask]


def prefix_call(records, entering):
    return kernel_call(
        prefix_kernel,
        [("vmem", records), ("vmem", entering)],
        [("vmem", (ROWS, WIDTH), BF16)] * OWNERS,
        [pltpu.VMEM(records.shape, BF16)],
        "prefix",
        0,
        2 << 20,
    )


def far_kernel(mine, slots, sources, *refs):
    near, enter_ref, (out_ref, ready, sems) = refs[: 3 * sources], refs[3 * sources], refs[-3:]
    copies = []
    for local, (source, slot) in enumerate(slots):
        query_ref, num_ref, stat_ref = near[3 * source : 3 * source + 3]
        mid, wide = slice(slot * DK, (slot + 1) * DK), slice(slot * DV, (slot + 1) * DV)
        at = local * PIECES
        aux = enter_ref[at, DK:ROWS]
        _, far_log, _ = read_aux(aux)
        far_log = far_log[:, 0:1]
        query = query_ref[:, mid]
        den = stat_ref[slot, 0:1]
        near_peak = stat_ref[slot, 1:2]
        peak = jnp.maximum(near_peak, far_log)
        near_part = jnp.exp(near_peak - peak)
        far_part = jnp.exp(far_log - peak) * SCALE
        below = near_part * den + far_part * dot_norm(aux, query)
        scale = 1.0 / jnp.maximum(jnp.abs(below), 1.0)
        near_column = column(near_part * scale)
        far_column = column(far_part * scale)
        memory = jnp.concatenate([enter_ref[at + piece, 0:DK] for piece in range(PIECES)], axis=1)
        for t in range(0, BLK, TILE):
            far = jnp.dot(query[t : t + TILE], memory, preferred_element_type=F32)
            near_weight = widen(near_column[t : t + TILE], DV)
            far_weight = widen(far_column[t : t + TILE], DV)
            near_rows = num_ref[t : t + TILE, wide].astype(F32)
            ready[local, t : t + TILE] = (near_weight * near_rows + far_weight * far).astype(BF16)
        head = first_head(mine, 0) + local
        copies.append(pltpu.make_async_copy(ready.at[local], out_ref.at[:, span(head, DV)], sems.at[local]))
        copies[-1].start()
    for copy in copies:
        copy.wait()


def far_call(mine, near, entering, out=None):
    slots, operands = [], []
    for source, (heads, results) in enumerate(near):
        operands += results
        slots += [(local, (source, slot)) for slot, (side, local) in enumerate(heads) if side == mine]
    slots = [slot for _, slot in sorted(slots)]
    operands = [pltpu.with_memory_space_constraint(x, pltpu.VMEM) for x in operands + [entering]]
    in_specs = [VMEM_SPEC] * len(operands)
    aliases = {}
    if out is not None:
        in_specs.append(pl.BlockSpec(memory_space=pltpu.HBM))
        aliases = {len(operands): 0}
        operands.append(out)
    return pl.pallas_call(
        functools.partial(far_kernel, mine, slots, len(near)),
        in_specs=in_specs,
        out_specs=pl.BlockSpec(memory_space=pltpu.HBM),
        out_shape=jax.ShapeDtypeStruct((BLK, HEADS * DV), BF16),
        scratch_shapes=[pltpu.VMEM((LOCAL, BLK, DV), BF16), pltpu.SemaphoreType.DMA((LOCAL,))],
        input_output_aliases=aliases,
        compiler_params=pltpu.CompilerParams(vmem_limit_bytes=8 << 20),
        name="far",
        cost_estimate=pl.CostEstimate(
            flops=LOCAL * 2 * BLK * DK * DV, transcendentals=0, bytes_accessed=LOCAL * 5 << 20
        ),
    )(*operands)


def on_device(query_raw, key_raw, values, in_gate, forget_gate, query_conv, key_conv):
    devices = lax.axis_size(AXES)
    cube_size = 2 * OWNERS
    cubes = devices // cube_size
    line = [(i, i + 1) for i in range(devices - 1)]
    swap = [(i, i ^ 1) for i in range(devices)]
    up = lambda distance: [(i, i + distance * cube_size) for i in range(devices - distance * cube_size)]
    after = lambda x, *done: lax.optimization_barrier((x,) + done)[0]

    def spread(records):
        moved = {0: records[0]}
        for mask in ORDER:
            route = [(i, i ^ (2 * mask)) for i in range(devices)]
            moved[mask] = lax.ppermute(records[mask], AXES, route)
        return [moved[mask] for mask in range(OWNERS)]

    rim = lax.ppermute(tails_call(key_raw, query_raw), AXES, line)
    rows, key_held, taps_held, val_held = prepare_call(in_gate, forget_gate, key_raw, key_conv, values)
    near_args = (query_raw, key_raw, rim, query_conv, key_conv, values)

    late = late_state_call(key_held, taps_held, val_held, rows)
    sent = early_state_call(key_held, rim, taps_held, val_held, rows, *late)
    rows = after(rows, sent)
    other = lax.ppermute(sent, AXES, swap)
    own, key_act = state_call(key_held, rim, taps_held, val_held, rows)
    joined = join_call(own, other)
    rows = after(rows, joined[0])
    records = spread(joined)
    *near_first, first = near_call(PARTS[0], *near_args, rows, (own, other, key_act))
    records[0] = after(records[0], near_first[0])
    stack, total = total_call(records)
    rows = after(rows, total)
    entering = lax.ppermute(total, AXES, up(1))
    distance = 1
    while distance < cubes - 1:
        earlier = lax.ppermute(entering, AXES, up(distance))
        entering = total_call([earlier, entering], (distance, 0))[1]
        distance *= 2
    near_second = near_call(PARTS[1], *near_args, rows)
    before = prefix_call(after(stack, near_second[0]), entering)
    rows = after(rows, before[0])
    records = spread(before)
    near_third = near_call(PARTS[2], *near_args, rows)
    records[0] = after(records[0], near_third[0])
    keep, send = split_call(records, first)
    enter_theirs = lax.ppermute(send, AXES, swap)
    near = list(zip(PARTS, ([*near_first], [*near_second], [*near_third])))
    sides = [[part for part in near if any(side == mine for side, _ in part[0])] for mine in (True, False)]
    out = far_call(True, sides[0], keep)
    return far_call(False, sides[1], enter_theirs, out)


def solution(mesh):
    split = P(AXES, None)
    in_specs = (split, split, split, split, split, P(), P())
    return jax.shard_map(on_device, mesh=mesh, in_specs=in_specs, out_specs=split, check_vma=False)
```
